128 devices in a mesh: dp: 32 (over x, y, core), tensor: 4 (over z).
Axes of the slice: x: 4, y: 4, z: 4, core: 2. Of those that a mesh axis runs over, the one named last changes fastest.
Arguments:
- activations: bfloat16 [65536, 8192], P('dp', 'tensor'), may hold values from -16 to 16
- whitening: bfloat16 [8192, 1024], P('tensor'), may hold values from -8 to 8
- factor: bfloat16 [1024, 1024], P(('dp', 'tensor')), may hold values from -2 to 2
Outputs:
- new_factor: float32 [1024, 1024], P(('dp', 'tensor'))
The draws below stay inside these ranges and needn't reach their ends.
All inputs are finite; a program needn't handle non-finite values.
Results may differ from the reference program's by a relative error of at most 0.029.
Values may be sent and summed in bfloat16 or wider, within the bound.
A program may use at most 192 MiB of HBM per device.

```python
import math
import jax
import jax.numpy as jnp
from jax import lax

W = 8192
R = 1024
K = 1024
TOK_DEV = 2048
TOKENS = 65536
N_DP = 32
N_TENSOR = 4


def feature_log_scale(key):
    reach = 0.5 * math.log(10.0)
    return jax.random.uniform(jax.random.fold_in(key, 7), (W,), jnp.float32, -reach, reach)


def draw_activations(key, part):
    feature = jnp.exp(feature_log_scale(key))
    noise_key = jax.random.fold_in(key, 13)
    base = jnp.clip(jax.random.normal(noise_key, (TOKENS, W), jnp.float32), -5.0, 5.0)
    return (base * feature[None, :]).astype(jnp.bfloat16)


def draw_whitening(key, part):
    log_scale = feature_log_scale(key)
    columns = jnp.arange(R, dtype=jnp.float32) / (R - 1)
    direction = jnp.where(jax.random.uniform(jax.random.fold_in(key, 19), (), jnp.float32) < 0.5, -1.0, 1.0)
    jitter = jax.random.uniform(jax.random.fold_in(key, 21), (R,), jnp.float32, -0.5, 0.5)
    tilt = jnp.clip(direction * (2.0 * columns - 1.0) + jitter, -1.0, 1.0)
    bend = jnp.exp(-0.75 * log_scale[:, None] * tilt[None, :])
    base_key = jax.random.fold_in(key, 17)
    base = jnp.clip(jax.random.normal(base_key, (W, R), jnp.float32), -6.0, 6.0)
    amplitude = jnp.exp(columns * math.log(4.0))
    return (base * bend * amplitude[None, :] * W ** (-0.5)).astype(jnp.bfloat16)


def draw_factor(key, part):
    first_key = jax.random.fold_in(key, 11)
    second_key = jax.random.fold_in(key, 23)
    other_key = jax.random.fold_in(key, 29)
    order_key = jax.random.fold_in(key, 31)
    mix_key = jax.random.fold_in(key, 37)
    order = jax.random.permutation(order_key, K).astype(jnp.int32)
    position = jnp.arange(K, dtype=jnp.int32)
    partner = jnp.zeros((K,), jnp.int32).at[order].set(order[position ^ 1])
    leader = jnp.zeros((K,), jnp.int32).at[order].set(1 - position % 2)
    mixing = jax.random.uniform(mix_key, (K,), jnp.float32, 0.8, 0.95)
    first = jnp.clip(jax.random.normal(first_key, (R, K), jnp.float32), -6.0, 6.0)
    other = jnp.clip(jax.random.normal(other_key, (R, K), jnp.float32), -6.0, 6.0)
    column_scale = jnp.exp(jax.random.uniform(second_key, (K,), jnp.float32, 0.0, 0.5 * math.log(10.0)))
    follower = mixing[None, :] * first[:, partner] + jnp.sqrt(1.0 - mixing * mixing)[None, :] * other
    base = jnp.where(leader[None, :] == 1, first, follower)
    base = jnp.clip(base, -6.0, 6.0)
    return (base * column_scale[None, :] * R ** (-0.5)).astype(jnp.bfloat16)


def setup_inputs(seed: int = 0) -> dict:
    streams_of = jax.random.split(jax.random.key(seed), 4)
    return {
        "activations": draw_activations(jax.random.fold_in(streams_of[3], 71), 0),
        "whitening": draw_whitening(jax.random.fold_in(streams_of[3], 71), 0),
        "factor": draw_factor(jax.random.fold_in(streams_of[3], 71), 0),
    }


ridge_shift = 0.1
epsilon = 1e-06

def solve_rows(moment_rows, hadamard):
    lower = jnp.linalg.cholesky(hadamard)
    first = jax.scipy.linalg.solve_triangular(lower, moment_rows.T, lower=True)
    second = jax.scipy.linalg.solve_triangular(lower, first, lower=True, trans=1)
    return second.T

def reference(activations, whitening, factor):
    width_part = W // N_TENSOR
    blocks = activations.reshape(N_DP, TOK_DEV, W)

    def accumulate(moment, block):
        summed = jnp.zeros((TOK_DEV, R), jnp.float32)
        for index in range(N_TENSOR):
            term = jnp.dot(block[:, index * width_part:(index + 1) * width_part].astype(jnp.float32), whitening[index * width_part:(index + 1) * width_part, :].astype(jnp.float32), preferred_element_type=jnp.float32)
            rounded = lax.optimization_barrier(term.astype(jnp.bfloat16))
            summed = summed + rounded.astype(jnp.float32)
        whitened = summed.astype(jnp.bfloat16)
        projected = jnp.dot(whitened.astype(jnp.float32), factor.astype(jnp.float32), preferred_element_type=jnp.float32)
        squared = (projected * projected).astype(jnp.bfloat16)
        moment = moment + jnp.dot(whitened.T.astype(jnp.float32), squared.astype(jnp.float32), preferred_element_type=jnp.float32)
        return (moment, None)
    moment, unused = lax.scan(accumulate, jnp.zeros((R, K), jnp.float32), blocks)
    gram = jnp.dot(factor.T.astype(jnp.float32), factor.astype(jnp.float32), preferred_element_type=jnp.float32)
    hadamard = gram * gram + ridge_shift * jnp.eye(K, dtype=jnp.float32)
    updated = solve_rows(moment, hadamard)
    column_total = lax.optimization_barrier(jnp.sum(updated * updated, axis=0))
    scale = jnp.sqrt(column_total / R + epsilon)
    return updated / scale[None, :]
```

```python
import jax, jax.numpy as jnp
from jax import lax
from jax.sharding import PartitionSpec as P
from jax.experimental import pallas as pl
from jax.experimental.pallas import tpu as pltpu

F32, BF16 = jnp.float32, jnp.bfloat16
HI = lax.Precision.HIGHEST

def over_lanes(x, j):
    return jnp.broadcast_to(x[:, j:j + 1], (8, 128))

def over_sublanes(x, j):
    return jnp.broadcast_to(x[j:j + 1, :], (8, 128))

def invert_block(rows):
    lane = lax.broadcasted_iota(jnp.int32, (8, 128), 1)
    sub = lax.broadcasted_iota(jnp.int32, (8, 128), 0)
    count = len(rows)
    for s in range(count):
        inside = (lane >= 8 * s) & (lane < 8 * s + 8)
        panel = rows[s]
        cols = [over_lanes(panel, 8 * s + j) for j in range(8)]
        z = jnp.where(inside, jnp.where(lane - 8 * s == sub, 1.0, 0.0), panel)
        for m in range(4):
            a, b = 2 * m, 2 * m + 1
            ea, eb = cols[a], cols[b]
            g00, g10 = over_sublanes(ea, a), over_sublanes(ea, b)
            g01, g11 = over_sublanes(eb, a), over_sublanes(eb, b)
            r = 1.0 / (g00 * g11 - g01 * g10)
            q00, q01, q10, q11 = g11 * r, -g01 * r, -g10 * r, g00 * r
            fa = -(ea * q00 + eb * q10)
            fb = -(ea * q01 + eb * q11)
            fa = jnp.where(sub == a, q00, jnp.where(sub == b, q10, fa))
            fb = jnp.where(sub == a, q01, jnp.where(sub == b, q11, fb))
            pair = (sub == a) | (sub == b)

            def step(v):
                return (jnp.where(pair, 0.0, v) + fa * over_sublanes(v, a)) + fb * over_sublanes(v, b)

            z = step(z)
            for c in range(b + 1, 8):
                cols[c] = step(cols[c])
        trow = [over_sublanes(z, j) for j in range(8)]
        for i in range(count):
            if i != s:
                v = rows[i]
                p = [over_lanes(v, 8 * s + j) * trow[j] for j in range(8)]
                total = ((p[0] + p[1]) + (p[2] + p[3])) + ((p[4] + p[5]) + (p[6] + p[7]))
                rows[i] = jnp.where(inside, 0.0, v) - total
        rows[s] = z
    return rows

def split(x):
    one = x.astype(BF16)
    rest = x - one.astype(F32)
    two = rest.astype(BF16)
    three = (rest - two.astype(F32)).astype(BF16)
    return one, two, three

def inverse_kernel(f_ref, a_ref, inv_ref, left, right):
    n = 1024
    for j in range(4):
        g = lax.dot_general(f_ref[:, 256 * j:256 * j + 256], f_ref[...], (((0,), (0,)), ((), ())), preferred_element_type=F32)
        row = lax.broadcasted_iota(jnp.int32, (256, n), 0) + 256 * j
        col = lax.broadcasted_iota(jnp.int32, (256, n), 1)
        h = g * g + jnp.where(row == col, 0.1, 0.0)
        a_ref[256 * j:256 * j + 256, :] = h
        inv_ref[256 * j:256 * j + 256, :] = h

    def step(k, carry):
        k0 = pl.multiple_of(k * 128, 128)
        block = [inv_ref[pl.ds(pl.multiple_of(k0 + 8 * i, 8), 8), pl.ds(k0, 128)] for i in range(16)]
        p = jnp.concatenate(invert_block(block), axis=0)
        panel = inv_ref[pl.ds(k0, 128), :]
        t = jnp.dot(p, panel, precision=HI, preferred_element_type=F32)
        inv_ref[pl.ds(k0, 128), :] = t
        inv_ref[pl.ds(k0, 128), pl.ds(k0, 128)] = p
        t1, t2, t3 = split(inv_ref[pl.ds(k0, 128), :])
        for i, piece in enumerate((t1, t2, t1, t3, t2, t1)):
            right[128 * i:128 * i + 128, :] = piece
        row = lax.broadcasted_iota(jnp.int32, (n, 128), 0)
        own = (row >= k0) & (row < k0 + 128)
        c = jnp.where(own, 0.0, inv_ref[:, pl.ds(k0, 128)])
        c1, c2, c3 = split(c)
        for i, piece in enumerate((c1, c1, c2, c1, c2, c3)):
            left[:, 128 * i:128 * i + 128] = piece
        inv_ref[:, pl.ds(k0, 128)] = jnp.where(own, inv_ref[:, pl.ds(k0, 128)], 0.0)
        for r in range(4):
            rows = slice(256 * r, 256 * r + 256)
            inv_ref[rows, :] -= jnp.dot(left[rows, :], right[...], preferred_element_type=F32)
        return carry

    lax.fori_loop(0, n // 128, step, 0)

def inverse(f):
    n = 1024
    return pl.pallas_call(
        inverse_kernel,
        out_shape=(jax.ShapeDtypeStruct((n, n), F32), jax.ShapeDtypeStruct((n, n), F32)),
        in_specs=[pl.BlockSpec(memory_space=pltpu.VMEM)],
        out_specs=(pl.BlockSpec(memory_space=pltpu.VMEM), pl.BlockSpec(memory_space=pltpu.VMEM)),
        scratch_shapes=[pltpu.VMEM((n, 768), BF16), pltpu.VMEM((768, n), BF16)],
        compiler_params=pltpu.CompilerParams(vmem_limit_bytes=40 * 2**20),
    )(f)

MESH = pl.DeviceIdType.MESH

def place():
    dp, z = lax.axis_index("dp"), lax.axis_index("tensor")
    return dp // 8, (dp // 2) % 4, dp % 2, z

def peer(x, y, c, z, d):
    px = lax.rem(x + d // 16, 4)
    py = lax.rem(y + lax.rem(d // 4, 4), 4)
    pz = lax.rem(z + lax.rem(d, 4), 4)
    return (px, py, pz), ((px * 4 + py) * 2 + c, pz)

def greet(x, y, c, z):
    barrier = pltpu.get_barrier_semaphore()

    def one(d, carry):
        _, device = peer(x, y, c, z, d)
        pl.semaphore_signal(barrier, inc=1, device_id=device, device_id_type=MESH)
        return carry

    lax.fori_loop(1, 64, one, 0)
    pl.semaphore_signal(barrier, inc=1, device_id=((x * 4 + y) * 2 + 1 - c, z), device_id_type=MESH)
    return barrier

def gather_kernel(f_ref, out_ref, send, recv, core_send, core_recv, own):
    x, y, c, z = place()
    barrier = greet(x, y, c, z)
    home = out_ref.at[x * 4 + y, c, z]
    copy_in = pltpu.make_async_copy(f_ref, home, own)
    copy_in.start()
    pl.semaphore_wait(barrier, 64)

    def put(d):
        _, device = peer(x, y, c, z, d)
        return pltpu.make_async_remote_copy(
            src_ref=f_ref, dst_ref=home, send_sem=send.at[d], recv_sem=recv.at[d], device_id=device, device_id_type=MESH)

    def start(d, carry):
        put(d).start()
        return carry

    def finish(d, carry):
        put(d).wait()
        return carry

    lax.fori_loop(1, 64, start, 0)
    copy_in.wait()
    lax.fori_loop(1, 64, finish, 0)
    half = out_ref.at[:, c]
    across = pltpu.make_async_remote_copy(
        src_ref=half, dst_ref=half, send_sem=core_send, recv_sem=core_recv,
        device_id=((x * 4 + y) * 2 + 1 - c, z), device_id_type=MESH)
    across.start()
    across.wait()

def gather(f):
    return pl.pallas_call(
        gather_kernel,
        out_shape=jax.ShapeDtypeStruct((16, 2, 4, 8, 1024), BF16),
        in_specs=[pl.BlockSpec(memory_space=pltpu.VMEM)],
        out_specs=pl.BlockSpec(memory_space=pltpu.VMEM),
        scratch_shapes=[pltpu.SemaphoreType.DMA((64,)), pltpu.SemaphoreType.DMA((64,)),
                        pltpu.SemaphoreType.DMA, pltpu.SemaphoreType.DMA, pltpu.SemaphoreType.DMA],
        compiler_params=pltpu.CompilerParams(collective_id=0, has_side_effects=True),
    )(f)

def finish_kernel(m_ref, inv_ref, out_ref, core_out, core_in, mine, parts, norm_out, norm_in,
                  send, recv, core_send, core_recv, nsend, nrecv, ncore_send, ncore_recv):
    x, y, c, z = place()
    barrier = greet(x, y, c, z)
    partner = ((x * 4 + y) * 2 + 1 - c, z)

    def cast(i, carry):
        core_out[i] = m_ref[i, 1 - c].astype(BF16)
        return carry

    lax.fori_loop(0, 16, cast, 0)
    pl.semaphore_wait(barrier, 64)
    across = pltpu.make_async_remote_copy(
        src_ref=core_out, dst_ref=core_in, send_sem=core_send, recv_sem=core_recv, device_id=partner, device_id_type=MESH)
    across.start()
    across.wait()

    def add(i, carry):
        mine[i] = (m_ref[i, c] + core_in[i].astype(F32)).astype(BF16)
        return carry

    lax.fori_loop(0, 16, add, 0)

    def put(d):
        (px, py, pz), device = peer(x, y, c, z, d)
        return pltpu.make_async_remote_copy(
            src_ref=mine.at[px * 4 + py, pz], dst_ref=parts.at[d], send_sem=send.at[d], recv_sem=recv.at[d],
            device_id=device, device_id_type=MESH)

    def start(d, carry):
        put(d).start()
        return carry

    def finish(d, total):
        put(d).wait()
        return total + parts[d].astype(F32)

    lax.fori_loop(1, 64, start, 0)
    home = x * 4 + y
    total = m_ref[home, c, z] + core_in[home, z].astype(F32)
    total = lax.fori_loop(1, 64, finish, total)
    updated = jnp.dot(total, inv_ref[...], precision=HI, preferred_element_type=F32)
    squares = jnp.sum(updated * updated, axis=0, keepdims=True)
    for j in range(8):
        norm_out[0, j:j + 1, :] = squares[:, 128 * j:128 * j + 128]
    ncore = pltpu.make_async_remote_copy(
        src_ref=norm_out.at[0], dst_ref=norm_in.at[0], send_sem=ncore_send, recv_sem=ncore_recv, device_id=partner, device_id_type=MESH)
    ncore.start()
    ncore.wait()
    norm_out[1] = norm_out[0] + norm_in[0]

    def nput(d):
        _, device = peer(x, y, c, z, d)
        return pltpu.make_async_remote_copy(
            src_ref=norm_out.at[1], dst_ref=norm_in.at[d], send_sem=nsend.at[d], recv_sem=nrecv.at[d],
            device_id=device, device_id_type=MESH)

    def nstart(d, carry):
        nput(d).start()
        return carry

    def nfinish(d, total):
        nput(d).wait()
        return total + norm_in[d]

    lax.fori_loop(1, 64, nstart, 0)
    norm = lax.fori_loop(1, 64, nfinish, norm_out[1])
    inverse_scale = 1.0 / jnp.sqrt(norm * (1.0 / 1024) + 1e-6)
    for j in range(8):
        out_ref[:, 128 * j:128 * j + 128] = updated[:, 128 * j:128 * j + 128] * inverse_scale[j:j + 1, :]

def finish(m, inv):
    return pl.pallas_call(
        finish_kernel,
        out_shape=jax.ShapeDtypeStruct((8, 1024), F32),
        in_specs=[pl.BlockSpec(memory_space=pltpu.VMEM)] * 2,
        out_specs=pl.BlockSpec(memory_space=pltpu.VMEM),
        scratch_shapes=[
            pltpu.VMEM((16, 4, 8, 1024), BF16), pltpu.VMEM((16, 4, 8, 1024), BF16), pltpu.VMEM((16, 4, 8, 1024), BF16),
            pltpu.VMEM((64, 8, 1024), BF16), pltpu.VMEM((2, 8, 128), F32), pltpu.VMEM((64, 8, 128), F32),
            pltpu.SemaphoreType.DMA((64,)), pltpu.SemaphoreType.DMA((64,)), pltpu.SemaphoreType.DMA, pltpu.SemaphoreType.DMA,
            pltpu.SemaphoreType.DMA((64,)), pltpu.SemaphoreType.DMA((64,)), pltpu.SemaphoreType.DMA, pltpu.SemaphoreType.DMA],
        compiler_params=pltpu.CompilerParams(collective_id=1, has_side_effects=True, vmem_limit_bytes=40 * 2**20),
    )(m, inv)


def shards(activations, whitening, factor):
    partial = jnp.dot(activations, whitening, preferred_element_type=F32).astype(BF16)
    summed = lax.psum_scatter(partial, "tensor", scatter_dimension=0, tiled=True)
    whole_factor = gather(factor).reshape(1024, 1024)
    hadamard, inv = inverse(whole_factor)
    projected = jnp.dot(summed, whole_factor, preferred_element_type=F32)
    squared = (projected * projected).astype(BF16)
    moment = lax.dot_general(summed, squared, (((0,), (0,)), ((), ())), preferred_element_type=F32)
    return finish(moment.reshape(16, 2, 4, 8, 1024), inv)


def solution(mesh):
    placed = (P("dp", "tensor"), P("tensor", None), P(("dp", "tensor"), None))
    return jax.shard_map(
        shards, mesh=mesh, in_specs=placed, out_specs=P(("dp", "tensor"), None), check_vma=False
    )
```

```python
import jax, jax.numpy as jnp
from jax import lax
from jax.sharding import PartitionSpec as P
from jax.experimental import pallas as pl
from jax.experimental.pallas import tpu as pltpu

F32, BF16 = jnp.float32, jnp.bfloat16
HI = lax.Precision.HIGHEST

def over_lanes(x, j):
    return jnp.broadcast_to(x[:, j:j + 1], (8, 128))

def over_sublanes(x, j):
    return jnp.broadcast_to(x[j:j + 1, :], (8, 128))

def tree(p):
    while len(p) > 1:
        p = [p[i] + p[i + 1] for i in range(0, len(p), 2)]
    return p[0]

def eliminate(rows, cols, first, s, lane, sub):
    base = first + 8 * s
    more = s + 1 < len(rows)
    inside = (lane >= base) & (lane < base + 8)
    panel = rows[s]
    if cols is None:
        cols = [over_lanes(panel, base + j) for j in range(8)]
    cols = list(cols)
    z = jnp.where(inside, jnp.where(lane - base == sub, 1.0, 0.0), panel)
    ahead = [over_lanes(panel, base + 8 + j) for j in range(8)] if more else []
    for m in range(4):
        a, b = 2 * m, 2 * m + 1
        ea, eb = cols[a], cols[b]
        g00, g10 = over_sublanes(ea, a), over_sublanes(ea, b)
        g01, g11 = over_sublanes(eb, a), over_sublanes(eb, b)
        r = 1.0 / (g00 * g11 - g01 * g10)
        q00, q01, q10, q11 = g11 * r, -(g01 * r), -(g10 * r), g00 * r
        fa = -(ea * q00 + eb * q10)
        fb = -(ea * q01 + eb * q11)
        fa = jnp.where(sub == a, q00, jnp.where(sub == b, q10, fa))
        fb = jnp.where(sub == a, q01, jnp.where(sub == b, q11, fb))
        pair = (sub == a) | (sub == b)

        def step(v):
            return (jnp.where(pair, 0.0, v) + fa * over_sublanes(v, a)) + fb * over_sublanes(v, b)

        for c in range(b + 1, 8):
            cols[c] = step(cols[c])
        z = step(z)
        ahead = [step(v) for v in ahead]
    following = None
    trow = [over_sublanes(z, j) for j in range(8)]
    for i in list(range(s + 1, len(rows))) + list(range(s)):
        v = rows[i]
        spread = [over_lanes(v, base + j) for j in range(8)]
        if i == s + 1:
            following = [
                over_lanes(v, base + 8 + j) - tree([spread[m] * over_sublanes(ahead[j], m) for m in range(8)])
                for j in range(8)]
        rows[i] = jnp.where(inside, 0.0, v) - tree([spread[j] * trow[j] for j in range(8)])
    rows[s] = z
    return following

def invert_block(rows, size, fill):
    lane = lax.broadcasted_iota(jnp.int32, (8, 128), 1)
    sub = lax.broadcasted_iota(jnp.int32, (8, 128), 0)
    each = size // 8
    groups = 128 // size
    zero = [jnp.zeros((8, 128), F32)]
    for g in range(groups):
        own = rows[each * g:each * g + each]
        cols = None
        for s in range(each):
            cols = eliminate(own, cols, size * g, s, lane, sub)
            fill()
        rows[each * g:each * g + each] = own
        inside = (lane >= size * g) & (lane < size * g + size)
        t = jnp.concatenate(zero * (each * g) + own + zero * (16 - each * g - each), axis=0)
        for o in [(g + e) % groups for e in range(1, groups)]:
            c = jnp.concatenate([jnp.where(inside, rows[i], 0.0) for i in range(each * o, each * o + each)], axis=0)
            u = jnp.dot(c, t, precision=HI, preferred_element_type=F32)
            for n in range(each):
                i = each * o + n
                rows[i] = jnp.where(inside, 0.0, rows[i]) - u[8 * n:8 * n + 8]
    return rows

TERMS = ((0, 0), (0, 1), (1, 0), (0, 2), (1, 1), (2, 0))
SIZE = 64
N = 1024

def split(x):
    one = x.astype(BF16)
    rest = x - one.astype(F32)
    two = rest.astype(BF16)
    three = (rest - two.astype(F32)).astype(BF16)
    return one, two, three

def hadamard_block(f_ref, i, rows, j, cols):
    g = lax.dot_general(f_ref[:, i:i + rows], f_ref[:, j:j + cols], (((0,), (0,)), ((), ())), preferred_element_type=F32)
    row = lax.broadcasted_iota(jnp.int32, (rows, cols), 0) + i
    col = lax.broadcasted_iota(jnp.int32, (rows, cols), 1) + j
    return g * g + jnp.where(row == col, 0.1, 0.0)

def invert(f_ref, inv_ref, left, right, pivot):
    def run(todo, rate):
        def fill():
            for _ in range(rate):
                if todo:
                    todo.pop(0)()
        return fill

    def fill_rows(j):
        def go():
            inv_ref[128 * j:128 * j + 128, :] = hadamard_block(f_ref, 128 * j, 128, 0, N)
        return go

    d = hadamard_block(f_ref, 0, 128, 0, 128)
    todo = [fill_rows(j) for j in range(8)]
    first = invert_block([d[8 * i:8 * i + 8] for i in range(16)], SIZE, run(todo, 1))
    pivot[...] = jnp.concatenate(first, axis=0)

    def work(k0):
        p = pivot[...]
        row = lax.broadcasted_iota(jnp.int32, (N, 128), 0)
        col = lax.broadcasted_iota(jnp.int32, (128, 256), 1)
        own = (row >= k0) & (row < k0 + 128)
        pp = jnp.concatenate([p, p], axis=1)

        def panel(j):
            def go():
                cols = slice(256 * j, 256 * j + 256)
                t = jnp.dot(p, inv_ref[pl.ds(k0, 128), cols], precision=HI, preferred_element_type=F32)
                at = col + 256 * j
                t = jnp.where((at >= k0) & (at < k0 + 128), pp, t)
                inv_ref[pl.ds(k0, 128), cols] = t
                tt = split(t)
                for i, (a, b) in enumerate(TERMS):
                    right[128 * i:128 * i + 128, cols] = tt[b]
            return go

        def column():
            old = inv_ref[:, pl.ds(k0, 128)]
            cc = split(jnp.where(own, 0.0, old))
            for i, (a, b) in enumerate(TERMS):
                left[:, 128 * i:128 * i + 128] = cc[a]
            inv_ref[:, pl.ds(k0, 128)] = jnp.where(own, old, 0.0)

        def update(r, c):
            def go():
                rows, cols = slice(128 * r, 128 * r + 128), slice(512 * c, 512 * c + 512)
                inv_ref[rows, cols] -= jnp.dot(left[rows, :], right[:, cols], preferred_element_type=F32)
            return go

        return [column] + [panel(j) for j in range(4)] + [update(r, c) for r in range(8) for c in range(2)]

    def step(k, carry):
        k0 = pl.multiple_of(k * 128, 128)
        n0 = pl.multiple_of(k * 128 + 128, 128)
        p = pivot[...]
        tn = jnp.dot(p, inv_ref[pl.ds(k0, 128), pl.ds(n0, 128)], precision=HI, preferred_element_type=F32)
        d = inv_ref[pl.ds(n0, 128), pl.ds(n0, 128)] - jnp.dot(
            inv_ref[pl.ds(n0, 128), pl.ds(k0, 128)], tn, precision=HI, preferred_element_type=F32)
        todo = work(k0)
        nxt = invert_block([d[8 * i:8 * i + 8] for i in range(16)], SIZE, run(todo, 2))
        while todo:
            todo.pop(0)()
        pivot[...] = jnp.concatenate(nxt, axis=0)
        return carry

    lax.fori_loop(0, N // 128 - 1, step, 0)
    for go in work(N - 128):
        go()


MESH = pl.DeviceIdType.MESH
OFFSETS = [(a, b, e) for a in range(4) for b in range(4) for e in range(4) if a + b + e > 0]


def ring(i):
    return [i] + [jnp.where(i + s >= 4, i + s - 4, i + s) for s in (1, 2, 3)]


class Map:
    def __init__(self):
        dp, z = lax.axis_index("dp"), lax.axis_index("tensor")
        x, y, self.c = dp // 8, (dp // 2) % 4, dp % 2
        xs, ys, self.zs = ring(x), ring(y), ring(z)
        self.pos = {o: (xs[o[0]] * 4 + ys[o[1]], self.zs[o[2]]) for o in OFFSETS}
        self.xy, self.z = x * 4 + y, z
        self.partner = (self.xy * 2 + 1 - self.c, z)

    def device(self, o):
        xy, z = self.pos[o]
        return (xy * 2 + self.c, z)


def greet(m):
    barrier = pltpu.get_barrier_semaphore()
    for o in OFFSETS:
        pl.semaphore_signal(barrier, inc=1, device_id=m.device(o), device_id_type=MESH)
    pl.semaphore_signal(barrier, inc=1, device_id=m.partner, device_id_type=MESH)
    return barrier


def remote(src, dst, send, recv, device):
    return pltpu.make_async_remote_copy(
        src_ref=src, dst_ref=dst, send_sem=send, recv_sem=recv, device_id=device, device_id_type=MESH)


def all_of(ref, sem):
    return pltpu.make_async_copy(ref, ref, sem)


def whole_kernel(act_ref, wh_ref, f_ref, out_ref,
                 act, wh, part, far, near, f5, factor, inv, left, right, pivot, summed, squared, moment,
                 core_out, core_in, mine, parts, norm_out, norm_in,
                 act_sem, wh_sem, f_send, f_recv, a_send, a_recv, n_send, n_recv, pair_send, pair_recv, far_send, far_recv, near_send, near_recv):
    m = Map()
    c, z = m.c, m.z
    barrier = greet(m)
    order = (m.zs[2], m.zs[1], m.zs[3], z)
    for r in range(4):
        rows = pl.ds(pl.multiple_of(order[r] * 512, 512), 512)
        pltpu.make_async_copy(act_ref.at[rows, :], act.at[r], act_sem.at[r]).start()
        if r == 0:
            pltpu.make_async_copy(wh_ref, wh, wh_sem).start()
    f5[m.xy, c, z] = f_ref[...]
    pl.semaphore_wait(barrier, 64)

    home = f5.at[m.xy, c, z]
    for o in OFFSETS:
        remote(f_ref, home, f_send, f_recv, m.device(o)).start()

    up, down = m.device((0, 0, 1)), m.device((0, 0, 3))
    far_up = remote(part.at[0, pl.ds(0, 256)], far.at[0], far_send.at[0], far_recv.at[0], up)
    far_down = remote(part.at[0, pl.ds(256, 256)], far.at[1], far_send.at[1], far_recv.at[1], down)
    near_up = remote(part.at[1], near.at[0], near_send.at[0], near_recv.at[0], up)
    near_down = remote(part.at[2], near.at[1], near_send.at[1], near_recv.at[1], down)
    pltpu.make_async_copy(wh_ref, wh, wh_sem).wait()
    for r in range(4):
        rows = pl.ds(pl.multiple_of(order[r] * 512, 512), 512)
        pltpu.make_async_copy(act_ref.at[rows, :], act.at[r], act_sem.at[r]).wait()

        def tile(i, carry, r=r):
            cols = pl.ds(pl.multiple_of(i * 256, 256), 256)
            part[r, :, cols] = jnp.dot(act[r], wh[:, cols], preferred_element_type=F32).astype(BF16)
            return carry

        lax.fori_loop(0, 4, tile, 0)
        if r == 0:
            far_up.start()
            far_down.start()

    all_of(parts, f_recv).wait()
    pair = remote(f5.at[:, c], f5.at[:, c], pair_send.at[0], pair_recv.at[0], m.partner)
    pair.start()

    far_up.wait_recv()

    def add_up(i, carry):
        rows = pl.ds(pl.multiple_of(i * 32, 32), 32)
        part[1, rows, :] = (part[1, rows, :].astype(F32) + far[0, rows, :].astype(F32)).astype(BF16)
        return carry

    lax.fori_loop(0, 8, add_up, 0)
    near_up.start()
    far_down.wait_recv()

    def add_down(i, carry):
        here = pl.ds(pl.multiple_of(i * 32, 32), 32)
        rows = pl.ds(pl.multiple_of(256 + i * 32, 32), 32)
        part[2, rows, :] = (part[2, rows, :].astype(F32) + far[1, here, :].astype(F32)).astype(BF16)
        return carry

    lax.fori_loop(0, 8, add_down, 0)
    near_down.start()
    pair.wait_recv()

    def flatten(i, carry):
        for e in range(2):
            for h in range(2):
                block = jnp.concatenate(
                    [f5[i, e, 2 * h].astype(F32), f5[i, e, 2 * h + 1].astype(F32)], axis=0)
                factor[pl.ds(pl.multiple_of(i * 64 + 32 * e + 16 * h, 16), 16), :] = block.astype(BF16)
        return carry

    lax.fori_loop(0, 16, flatten, 0)
    invert(factor, inv, left, right, pivot)

    near_up.wait_recv()
    near_down.wait_recv()

    def total_rows(i, carry):
        rows = pl.ds(pl.multiple_of(i * 32, 32), 32)
        summed[rows, :] = (part[3, rows, :].astype(F32) + near[0, rows, :].astype(F32)
                           + near[1, rows, :].astype(F32)).astype(BF16)
        return carry

    lax.fori_loop(0, 16, total_rows, 0)

    def project(i, carry):
        cols = pl.ds(pl.multiple_of(i * 256, 256), 256)
        p = jnp.dot(summed[...], factor[:, cols], preferred_element_type=F32)
        squared[:, cols] = (p * p).astype(BF16)
        return carry

    lax.fori_loop(0, 4, project, 0)

    def moments(i, carry):
        rows = pl.ds(pl.multiple_of(i * 256, 256), 256)
        moment[rows, :] = lax.dot_general(
            summed[:, rows], squared[...], (((0,), (0,)), ((), ())), preferred_element_type=F32)
        return carry

    lax.fori_loop(0, 4, moments, 0)

    def block(i, core):
        return moment[pl.ds(pl.multiple_of((i * 2 + core) * 32, 32), 32), :].reshape(4, 8, 1024)

    def cast(i, carry):
        core_out[i] = block(i, 1 - c).astype(BF16)
        return carry

    lax.fori_loop(0, 16, cast, 0)
    across = remote(core_out, core_in, pair_send.at[1], pair_recv.at[1], m.partner)
    across.start()
    across.wait_recv()

    def add(i, carry):
        mine[i] = (block(i, c) + core_in[i].astype(F32)).astype(BF16)
        return carry

    lax.fori_loop(0, 16, add, 0)
    for d, o in enumerate(OFFSETS):
        xy, pz = m.pos[o]
        remote(mine.at[xy, pz], parts.at[d], a_send, a_recv, m.device(o)).start()
    own_rows = pl.multiple_of(((m.xy * 2 + c) * 4 + z) * 8, 8)
    total = moment[pl.ds(own_rows, 8), :] + core_in[m.xy, z].astype(F32)
    all_of(parts, a_recv).wait()
    total = lax.fori_loop(0, 63, lambda d, t: t + parts[d].astype(F32), total)
    updated = jnp.dot(total, inv[...], precision=HI, preferred_element_type=F32)

    squares = jnp.sum(updated * updated, axis=0, keepdims=True)
    for j in range(8):
        norm_out[0, j:j + 1, :] = squares[:, 128 * j:128 * j + 128]
    between = remote(norm_out.at[0], norm_in.at[63], pair_send.at[2], pair_recv.at[2], m.partner)
    between.start()
    between.wait_recv()
    norm_out[1] = norm_out[0] + norm_in[63]
    for d, o in enumerate(OFFSETS):
        remote(norm_out.at[1], norm_in.at[d], n_send, n_recv, m.device(o)).start()
    all_of(norm_in.at[pl.ds(0, 63)], n_recv).wait()
    norm = norm_out[1]
    for d in range(63):
        norm = norm + norm_in[d]
    scale = jnp.sqrt(norm * (1.0 / N) + 1e-6)
    for j in range(8):
        cols = slice(128 * j, 128 * j + 128)
        out_ref[:, cols] = updated[:, cols] / scale[j:j + 1, :]
    all_of(parts, f_send).wait()
    all_of(parts, a_send).wait()
    all_of(norm_in.at[pl.ds(0, 63)], n_send).wait()
    for copy in (pair, across, between, far_up, far_down, near_up, near_down):
        copy.wait_send()


def shards(activations, whitening, factor):
    terms = 128 * len(TERMS)
    dma = pltpu.SemaphoreType.DMA
    return pl.pallas_call(
        whole_kernel,
        out_shape=jax.ShapeDtypeStruct((8, N), F32),
        in_specs=[pl.BlockSpec(memory_space=pl.ANY)] * 2 + [pl.BlockSpec(memory_space=pltpu.VMEM)],
        out_specs=pl.BlockSpec(memory_space=pltpu.VMEM),
        scratch_shapes=[
            pltpu.VMEM((4, 512, 2048), BF16), pltpu.VMEM((2048, N), BF16), pltpu.VMEM((4, 512, N), BF16),
            pltpu.VMEM((2, 256, N), BF16), pltpu.VMEM((2, 512, N), BF16),
            pltpu.VMEM((16, 2, 4, 8, N), BF16), pltpu.VMEM((N, N), BF16), pltpu.VMEM((N, N), F32),
            pltpu.VMEM((N, terms), BF16), pltpu.VMEM((terms, N), BF16), pltpu.VMEM((128, 128), F32),
            pltpu.VMEM((512, N), BF16), pltpu.VMEM((512, N), BF16), pltpu.VMEM((N, N), F32),
            pltpu.VMEM((16, 4, 8, N), BF16), pltpu.VMEM((16, 4, 8, N), BF16), pltpu.VMEM((16, 4, 8, N), BF16),
            pltpu.VMEM((63, 8, N), BF16), pltpu.VMEM((2, 8, 128), F32), pltpu.VMEM((64, 8, 128), F32),
            dma((4,)), dma, dma, dma, dma, dma, dma, dma, dma((3,)), dma((3,)), dma((2,)), dma((2,)), dma((2,)), dma((2,))],
        compiler_params=pltpu.CompilerParams(
            collective_id=0, has_side_effects=True, vmem_limit_bytes=56 * 2**20),
    )(activations, whitening, factor)


def solution(mesh):
    placed = (P("dp", "tensor"), P("tensor", None), P(("dp", "tensor"), None))
    return jax.shard_map(
        shards, mesh=mesh, in_specs=placed, out_specs=P(("dp", "tensor"), None), check_vma=False
    )
```

```python
import jax, jax.numpy as jnp
from jax import lax
from jax.sharding import PartitionSpec as P
from jax.experimental import pallas as pl
from jax.experimental.pallas import tpu as pltpu

F32, BF16 = jnp.float32, jnp.bfloat16
HI = lax.Precision.HIGHEST

def over_lanes(x, j):
    return jnp.broadcast_to(x[:, j:j + 1], (8, 128))

def over_sublanes(x, j):
    return jnp.broadcast_to(x[j:j + 1, :], (8, 128))

def tree(p):
    while len(p) > 1:
        p = [p[i] + p[i + 1] for i in range(0, len(p), 2)]
    return p[0]

def eliminate(rows, cols, first, s, lane, sub):
    base = first + 8 * s
    more = s + 1 < len(rows)
    inside = (lane >= base) & (lane < base + 8)
    panel = rows[s]
    if cols is None:
        cols = [over_lanes(panel, base + j) for j in range(8)]
    cols = list(cols)
    z = jnp.where(inside, jnp.where(lane - base == sub, 1.0, 0.0), panel)
    ahead = [over_lanes(panel, base + 8 + j) for j in range(8)] if more else []
    for m in range(4):
        a, b = 2 * m, 2 * m + 1
        ea, eb = cols[a], cols[b]
        g00, g10 = over_sublanes(ea, a), over_sublanes(ea, b)
        g01, g11 = over_sublanes(eb, a), over_sublanes(eb, b)
        r = 1.0 / (g00 * g11 - g01 * g10)
        q00, q01, q10, q11 = g11 * r, -(g01 * r), -(g10 * r), g00 * r
        fa = -(ea * q00 + eb * q10)
        fb = -(ea * q01 + eb * q11)
        fa = jnp.where(sub == a, q00, jnp.where(sub == b, q10, fa))
        fb = jnp.where(sub == a, q01, jnp.where(sub == b, q11, fb))
        pair = (sub == a) | (sub == b)

        def step(v):
            return (jnp.where(pair, 0.0, v) + fa * over_sublanes(v, a)) + fb * over_sublanes(v, b)

        for c in range(b + 1, 8):
            cols[c] = step(cols[c])
        z = step(z)
        ahead = [step(v) for v in ahead]
    following = None
    trow = [over_sublanes(z, j) for j in range(8)]
    for i in list(range(s + 1, len(rows))) + list(range(s)):
        v = rows[i]
        spread = [over_lanes(v, base + j) for j in range(8)]
        if i == s + 1:
            following = [
                over_lanes(v, base + 8 + j) - tree([spread[m] * over_sublanes(ahead[j], m) for m in range(8)])
                for j in range(8)]
        rows[i] = jnp.where(inside, 0.0, v) - tree([spread[j] * trow[j] for j in range(8)])
    rows[s] = z
    return following

def invert_block(rows, size, fill):
    lane = lax.broadcasted_iota(jnp.int32, (8, 128), 1)
    sub = lax.broadcasted_iota(jnp.int32, (8, 128), 0)
    each = size // 8
    groups = 128 // size
    zero = [jnp.zeros((8, 128), F32)]
    for g in range(groups):
        own = rows[each * g:each * g + each]
        cols = None
        for s in range(each):
            cols = eliminate(own, cols, size * g, s, lane, sub)
            fill()
        rows[each * g:each * g + each] = own
        inside = (lane >= size * g) & (lane < size * g + size)
        t = jnp.concatenate(zero * (each * g) + own + zero * (16 - each * g - each), axis=0)
        for o in [(g + e) % groups for e in range(1, groups)]:
            c = jnp.concatenate([jnp.where(inside, rows[i], 0.0) for i in range(each * o, each * o + each)], axis=0)
            u = jnp.dot(c, t, precision=HI, preferred_element_type=F32)
            for n in range(each):
                i = each * o + n
                rows[i] = jnp.where(inside, 0.0, rows[i]) - u[8 * n:8 * n + 8]
    return rows

TERMS = ((0, 0), (0, 1), (1, 0), (0, 2), (1, 1), (2, 0))
SIZE = 64
N = 1024

def split(x):
    one = x.astype(BF16)
    rest = x - one.astype(F32)
    two = rest.astype(BF16)
    three = (rest - two.astype(F32)).astype(BF16)
    return one, two, three

def hadamard_block(f_ref, i, rows, j, cols):
    g = lax.dot_general(f_ref[:, i:i + rows], f_ref[:, j:j + cols], (((0,), (0,)), ((), ())), preferred_element_type=F32)
    row = lax.broadcasted_iota(jnp.int32, (rows, cols), 0) + i
    col = lax.broadcasted_iota(jnp.int32, (rows, cols), 1) + j
    return g * g + jnp.where(row == col, 0.1, 0.0)

def invert(f_ref, inv_ref, left, right, pivot, between):
    def run(todo, rate):
        def fill():
            for _ in range(rate):
                if todo:
                    todo.pop(0)()
        return fill

    def fill_rows(j):
        def go():
            inv_ref[128 * j:128 * j + 128, :] = hadamard_block(f_ref, 128 * j, 128, 0, N)
        return go

    d = hadamard_block(f_ref, 0, 128, 0, 128)
    todo = [fill_rows(j) for j in range(8)]
    first = invert_block([d[8 * i:8 * i + 8] for i in range(16)], SIZE, run(todo, 1))
    pivot[...] = jnp.concatenate(first, axis=0)

    def work(k0):
        p = pivot[...]
        row = lax.broadcasted_iota(jnp.int32, (N, 128), 0)
        col = lax.broadcasted_iota(jnp.int32, (128, 256), 1)
        own = (row >= k0) & (row < k0 + 128)
        pp = jnp.concatenate([p, p], axis=1)

        def panel(j):
            def go():
                cols = slice(256 * j, 256 * j + 256)
                t = jnp.dot(p, inv_ref[pl.ds(k0, 128), cols], precision=HI, preferred_element_type=F32)
                at = col + 256 * j
                t = jnp.where((at >= k0) & (at < k0 + 128), pp, t)
                inv_ref[pl.ds(k0, 128), cols] = t
                tt = split(t)
                for i, (a, b) in enumerate(TERMS):
                    right[128 * i:128 * i + 128, cols] = tt[b]
            return go

        def column():
            old = inv_ref[:, pl.ds(k0, 128)]
            cc = split(jnp.where(own, 0.0, old))
            for i, (a, b) in enumerate(TERMS):
                left[:, 128 * i:128 * i + 128] = cc[a]
            inv_ref[:, pl.ds(k0, 128)] = jnp.where(own, old, 0.0)

        def update(r, c):
            def go():
                rows, cols = slice(128 * r, 128 * r + 128), slice(512 * c, 512 * c + 512)
                inv_ref[rows, cols] -= jnp.dot(left[rows, :], right[:, cols], preferred_element_type=F32)
            return go

        return [column] + [panel(j) for j in range(4)] + [update(r, c) for r in range(8) for c in range(2)]

    def step(k, carry):
        between(k)
        k0 = pl.multiple_of(k * 128, 128)
        n0 = pl.multiple_of(k * 128 + 128, 128)
        p = pivot[...]
        tn = jnp.dot(p, inv_ref[pl.ds(k0, 128), pl.ds(n0, 128)], precision=HI, preferred_element_type=F32)
        d = inv_ref[pl.ds(n0, 128), pl.ds(n0, 128)] - jnp.dot(
            inv_ref[pl.ds(n0, 128), pl.ds(k0, 128)], tn, precision=HI, preferred_element_type=F32)
        todo = work(k0)
        nxt = invert_block([d[8 * i:8 * i + 8] for i in range(16)], SIZE, run(todo, 2))
        while todo:
            todo.pop(0)()
        pivot[...] = jnp.concatenate(nxt, axis=0)
        return carry

    lax.fori_loop(0, N // 128 - 1, step, 0)
    for go in work(N - 128):
        go()


MESH = pl.DeviceIdType.MESH
PARTS = ((0, 384, (0, 1, 2)), (384, 384, (1, 2, 0)), (768, 256, (2, 0, 1)))
STAGES = (3, 4, 5, 6, None)


def ring(i):
    return [i] + [jnp.where(i + s >= 4, i + s - 4, i + s) for s in (1, 2, 3)]


class Map:
    def __init__(self):
        dp, z = lax.axis_index("dp"), lax.axis_index("tensor")
        self.c = dp % 2
        self.at = (dp // 8, (dp // 2) % 4, z)
        self.rings = [ring(i) for i in self.at]
        self.partner = self.name(self.at, 1 - self.c)

    def name(self, at, core):
        return ((at[0] * 4 + at[1]) * 2 + core, at[2])

    def peer(self, axis, s):
        at = list(self.at)
        at[axis] = self.rings[axis][s]
        return self.name(at, self.c)

    def close(self):
        x, y, _ = self.at
        zs = self.rings[2]
        return [self.name((x, y, zs[s]), core) for core in (self.c, 1 - self.c) for s in range(4) if core is not self.c or s]

    def plane(self):
        xs, ys, _ = self.rings
        return [self.name((xs[a], ys[b], self.at[2]), self.c) for a in range(4) for b in range(4) if a + b]


def greet(m):
    barrier = pltpu.get_barrier_semaphore()
    for device in m.close() + m.plane():
        pl.semaphore_signal(barrier, inc=1, device_id=device, device_id_type=MESH)
    return barrier


def remote(src, dst, send, recv, device):
    return pltpu.make_async_remote_copy(
        src_ref=src, dst_ref=dst, send_sem=send, recv_sem=recv, device_id=device, device_id_type=MESH)


def all_of(ref, sem):
    return pltpu.make_async_copy(ref, ref, sem)


def whole_kernel(act_ref, wh_ref, f_ref, out_ref,
                 act, wh, part, far, near, f5, factor, inv, left, right, pivot, summed, squared, moment,
                 core_out, core_in, mine, in1, out2, in2, out3, in3, total, norm_out, norm_in,
                 act_sem, wh_sem, f_send, f_recv, l_send, l_recv, s_send, s_recv, n_send, n_recv,
                 pair_send, pair_recv, far_send, far_recv, near_send, near_recv):
    m = Map()
    c = m.c
    x, y, z = m.at
    barrier = greet(m)
    zs = m.rings[2]
    order = (zs[2], zs[1], zs[3], z)

    def load(r):
        rows = pl.ds(pl.multiple_of(order[r] * 512, 512), 512)
        return pltpu.make_async_copy(act_ref.at[rows, :], act.at[r], act_sem.at[r])

    load_wh = pltpu.make_async_copy(wh_ref, wh, wh_sem)
    load_wh.start()
    for r in range(4):
        load(r).start()
    f5[x, y, c, z] = f_ref[...]
    pl.semaphore_wait(barrier, 22)

    first, second = pl.ds(0, 512), pl.ds(512, 512)
    hops = [
        (f_ref, f5.at[x, y, c, z], 2, f5.at[0, 0, 0, pl.ds(0, 3)]),
        (f5.at[x, y, c, :, :, first], f5.at[x, y, c, :, :, first], 0, f5.at[pl.ds(0, 3), 0, 0, :, :, first]),
        (f5.at[x, y, c, :, :, second], f5.at[x, y, c, :, :, second], 1, f5.at[pl.ds(0, 3), 0, 0, :, :, first]),
    ]

    def hop_start(i):
        src, dst, axis, _ = hops[i]
        for s in (1, 2, 3):
            remote(src, dst, f_send.at[i], f_recv.at[i], m.peer(axis, s)).start()

    def hop_end(i, sems):
        all_of(hops[i][3], sems.at[i]).wait()

    def strip(half, s):
        if half == 0:
            return f5.at[:, m.rings[1][s], c, :, :, first]
        return f5.at[x, :, c, :, :, second] if s == 0 else f5.at[m.rings[0][s], :, c, :, :, second]

    def last_hop(half, s):
        return remote(strip(half, 0), strip(half, 0), l_send.at[half, s - 1], l_recv.at[half, s - 1], m.peer(1 - half, s))

    def pair(half, s):
        return remote(strip(half, s), strip(half, s), pair_send.at[0], pair_recv.at[0], m.partner)

    hop_start(0)

    up, down = m.peer(2, 1), m.peer(2, 3)
    far_up = remote(part.at[0, pl.ds(0, 256)], far.at[0], far_send.at[0], far_recv.at[0], up)
    far_down = remote(part.at[0, pl.ds(256, 256)], far.at[1], far_send.at[1], far_recv.at[1], down)

    def near_copy(slot, half):
        rows = pl.ds(256 * half, 256)
        return remote(part.at[1 + slot, rows], near.at[slot, rows], near_send.at[slot, half], near_recv.at[slot, half],
                      down if slot else up)

    load_wh.wait()
    for r in range(4):
        load(r).wait()
        if r == 0:
            hop_end(0, f_recv)
            hop_start(1)
            hop_start(2)

        def tile(i, carry, r=r):
            cols = pl.ds(pl.multiple_of(i * 256, 256), 256)
            part[r, :, cols] = jnp.dot(act[r], wh[:, cols], preferred_element_type=F32).astype(BF16)
            return carry

        lax.fori_loop(0, 4, tile, 0)
        if r == 0:
            far_up.start()
            far_down.start()
            hop_end(1, f_recv)
            hop_end(2, f_recv)
            for s in (1, 2, 3):
                for half in (0, 1):
                    last_hop(half, s).start()
            for half in (0, 1):
                pair(half, 0).start()
        if r == 1:
            near_copy(0, 1).start()
        if r == 2:
            near_copy(1, 0).start()
            for s in (1, 3, 2):
                for half in (0, 1):
                    last_hop(half, s).wait_recv()
                    pair(half, 4 - s).start()

    def forward(copy_in, slot):
        begin = 256 * slot
        copy_in.wait_recv()

        def add(i, carry):
            here = pl.ds(pl.multiple_of(i * 32, 32), 32)
            rows = pl.ds(pl.multiple_of(begin + i * 32, 32), 32)
            part[1 + slot, rows, :] = (part[1 + slot, rows, :].astype(F32) + far[slot, here, :].astype(F32)).astype(BF16)
            return carry

        lax.fori_loop(0, 8, add, 0)
        near_copy(slot, slot).start()

    forward(far_up, 0)
    forward(far_down, 1)
    all_of(f5.at[:, :, 0], pair_recv.at[0]).wait()

    def flatten(i, carry):
        for e in range(2):
            for h in range(2):
                block = jnp.concatenate(
                    [f5[i // 4, i % 4, e, 2 * h].astype(F32), f5[i // 4, i % 4, e, 2 * h + 1].astype(F32)], axis=0)
                factor[pl.ds(pl.multiple_of(i * 64 + 32 * e + 16 * h, 16), 16), :] = block.astype(BF16)
        return carry

    lax.fori_loop(0, 16, flatten, 0)

    across = remote(core_out, core_in, pair_send.at[1], pair_recv.at[1], m.partner)

    def rows_of(i, core):
        return pl.ds(pl.multiple_of((i * 2 + core) * 32, 32), 32)

    def stage_moment():
        for slot in (0, 1):
            for half in (0, 1):
                near_copy(slot, half).wait_recv()

        def add(i, carry):
            rows = pl.ds(pl.multiple_of(i * 32, 32), 32)
            summed[rows, :] = (part[3, rows, :].astype(F32) + near[0, rows, :].astype(F32)
                               + near[1, rows, :].astype(F32)).astype(BF16)
            return carry

        lax.fori_loop(0, 16, add, 0)

        def project(i, carry):
            cols = pl.ds(pl.multiple_of(i * 256, 256), 256)
            p = jnp.dot(summed[...], factor[:, cols], preferred_element_type=F32)
            squared[:, cols] = (p * p).astype(BF16)
            return carry

        lax.fori_loop(0, 4, project, 0)

        def moments(i, carry):
            rows = pl.ds(pl.multiple_of(i * 256, 256), 256)
            moment[rows, :] = lax.dot_general(
                summed[:, rows], squared[...], (((0,), (0,)), ((), ())), preferred_element_type=F32)
            return carry

        lax.fori_loop(0, 4, moments, 0)

        def cast(i, carry):
            core_out[i] = moment[rows_of(i, 1 - c), :].reshape(4, 8, N).astype(BF16)
            return carry

        lax.fori_loop(0, 16, cast, 0)
        across.start()

    def pick(ref, fixed, cols):
        index = [fixed.get(axis, slice(None)) for axis in range(3)]
        return ref.at[(*index, slice(None), pl.ds(cols[0], cols[1]))]

    def send1(p, s):
        lo, width, (a, b, e) = PARTS[p]
        src = pick(mine, {a: m.rings[a][s]}, (lo, width))
        return remote(src, in1.at[s - 1, :, :, :, pl.ds(lo, width)], s_send.at[0, p], s_recv.at[0, p], m.peer(a, s))

    def send2(p, s):
        lo, width, (a, b, e) = PARTS[p]
        src = out2.at[m.rings[b][s], :, :, pl.ds(lo, width)]
        return remote(src, in2.at[s - 1, :, :, pl.ds(lo, width)], s_send.at[1, p], s_recv.at[1, p], m.peer(b, s))

    def send3(p, s):
        lo, width, (a, b, e) = PARTS[p]
        src = out3.at[m.rings[e][s], :, pl.ds(lo, width)]
        return remote(src, in3.at[s - 1, :, pl.ds(lo, width)], s_send.at[2, p], s_recv.at[2, p], m.peer(e, s))

    def landed(level, p, sems):
        lo, width, _ = PARTS[p]
        ref = (in1.at[:, :, :, :, pl.ds(lo, width)], in2.at[:, :, :, pl.ds(lo, width)], in3.at[:, :, pl.ds(lo, width)])[level]
        all_of(ref, sems.at[level, p]).wait()

    def stage_cores():
        across.wait_recv()

        def add(i, carry):
            block = moment[rows_of(i, c), :].reshape(4, 8, N) + core_in[i].astype(F32)
            moment[rows_of(i, c), :] = block.reshape(32, N)
            mine[i // 4, i % 4] = block.astype(BF16)
            return carry

        lax.fori_loop(0, 16, add, 0)
        for s in (1, 2, 3):
            for p in range(3):
                send1(p, s).start()

    def stage_one():
        for p in range(3):
            lo, width, (a, b, e) = PARTS[p]
            cols = pl.ds(lo, width)
            landed(0, p, s_recv)

            def add(i, carry):
                ib, ie = i // 4, i % 4
                index = [None] * 3
                index[a], index[b], index[e] = m.at[a], ib, ie
                row = pl.multiple_of((((index[0] * 4 + index[1]) * 2 + c) * 4 + index[2]) * 8, 8)
                j, k = (ib, ie) if b < e else (ie, ib)
                t = moment[pl.ds(row, 8), cols]
                for s in range(3):
                    t = t + in1[s, j, k, :, cols].astype(F32)
                moment[pl.ds(row, 8), cols] = t
                out2[ib, ie, :, cols] = t.astype(BF16)
                return carry

            lax.fori_loop(0, 16, add, 0)
            for s in (1, 2, 3):
                send2(p, s).start()

    def stage_two():
        for p in range(3):
            lo, width, (a, b, e) = PARTS[p]
            cols = pl.ds(lo, width)
            landed(1, p, s_recv)

            def add(ie, carry):
                index = list(m.at)
                index[e] = ie
                row = pl.multiple_of((((index[0] * 4 + index[1]) * 2 + c) * 4 + index[2]) * 8, 8)
                t = moment[pl.ds(row, 8), cols]
                for s in range(3):
                    t = t + in2[s, ie, :, cols].astype(F32)
                moment[pl.ds(row, 8), cols] = t
                out3[ie, :, cols] = t.astype(BF16)
                return carry

            lax.fori_loop(0, 4, add, 0)
            for s in (1, 2, 3):
                send3(p, s).start()

    def stage_three():
        own = pl.multiple_of((((x * 4 + y) * 2 + c) * 4 + z) * 8, 8)
        for p in range(3):
            lo, width, _ = PARTS[p]
            cols = pl.ds(lo, width)
            landed(2, p, s_recv)
            t = moment[pl.ds(own, 8), cols]
            for s in range(3):
                t = t + in3[s, :, cols].astype(F32)
            total[:, cols] = t

    stages = (stage_moment, stage_cores, stage_one, stage_two, stage_three)

    def between(k):
        for stage, when in zip(stages, STAGES):
            if when is not None:
                pl.when(k == when)(stage)

    invert(factor, inv, left, right, pivot, between)
    for stage, when in zip(stages, STAGES):
        if when is None:
            stage()
    updated = jnp.dot(total[...], inv[...], precision=HI, preferred_element_type=F32)

    squares = jnp.sum(updated * updated, axis=0, keepdims=True)
    for j in range(8):
        norm_out[0, j:j + 1, :] = squares[:, 128 * j:128 * j + 128]
    close, plane = m.close(), m.plane()
    for i, device in enumerate(close):
        remote(norm_out.at[0], norm_in.at[i], n_send.at[0], n_recv.at[0], device).start()
    all_of(norm_in.at[pl.ds(0, 7)], n_recv.at[0]).wait()
    norm = tree([norm_out[0]] + [norm_in[i] for i in range(7)])
    norm_out[1] = norm
    for i, device in enumerate(plane):
        remote(norm_out.at[1], norm_in.at[7 + i], n_send.at[1], n_recv.at[1], device).start()
    all_of(norm_in.at[pl.ds(7, 15)], n_recv.at[1]).wait()
    norm = tree([norm] + [norm_in[7 + i] for i in range(15)])
    scale = jnp.sqrt(norm * (1.0 / N) + 1e-6)
    for j in range(8):
        cols = slice(128 * j, 128 * j + 128)
        out_ref[:, cols] = updated[:, cols] / scale[j:j + 1, :]

    for i in range(3):
        hop_end(i, f_send)
    for s in (1, 2, 3):
        for half in (0, 1):
            last_hop(half, s).wait_send()
    for level in range(3):
        for p in range(3):
            landed(level, p, s_send)
    all_of(norm_in.at[pl.ds(0, 7)], n_send.at[0]).wait()
    all_of(norm_in.at[pl.ds(7, 15)], n_send.at[1]).wait()
    all_of(f5.at[:, :, 0], pair_send.at[0]).wait()
    for slot in (0, 1):
        for half in (0, 1):
            near_copy(slot, half).wait_send()
    for copy in (across, far_up, far_down):
        copy.wait_send()


def shards(activations, whitening, factor):
    terms = 128 * len(TERMS)
    dma = pltpu.SemaphoreType.DMA
    return pl.pallas_call(
        whole_kernel,
        out_shape=jax.ShapeDtypeStruct((8, N), F32),
        in_specs=[pl.BlockSpec(memory_space=pl.ANY)] * 2 + [pl.BlockSpec(memory_space=pltpu.VMEM)],
        out_specs=pl.BlockSpec(memory_space=pltpu.VMEM),
        scratch_shapes=[
            pltpu.VMEM((4, 512, 2048), BF16), pltpu.VMEM((2048, N), BF16), pltpu.VMEM((4, 512, N), BF16),
            pltpu.VMEM((2, 256, N), BF16), pltpu.VMEM((2, 512, N), BF16),
            pltpu.VMEM((4, 4, 2, 4, 8, N), BF16), pltpu.VMEM((N, N), BF16), pltpu.VMEM((N, N), F32),
            pltpu.VMEM((N, terms), BF16), pltpu.VMEM((terms, N), BF16), pltpu.VMEM((128, 128), F32),
            pltpu.VMEM((512, N), BF16), pltpu.VMEM((512, N), BF16), pltpu.VMEM((N, N), F32),
            pltpu.VMEM((16, 4, 8, N), BF16), pltpu.VMEM((16, 4, 8, N), BF16), pltpu.VMEM((4, 4, 4, 8, N), BF16),
            pltpu.VMEM((3, 4, 4, 8, N), BF16), pltpu.VMEM((4, 4, 8, N), BF16), pltpu.VMEM((3, 4, 8, N), BF16),
            pltpu.VMEM((4, 8, N), BF16), pltpu.VMEM((3, 8, N), BF16), pltpu.VMEM((8, N), F32),
            pltpu.VMEM((2, 8, 128), F32), pltpu.VMEM((22, 8, 128), F32),
            dma((4,)), dma, dma((3,)), dma((3,)), dma((2, 3)), dma((2, 3)), dma((3, 3)), dma((3, 3)), dma((2,)), dma((2,)),
            dma((2,)), dma((2,)), dma((2,)), dma((2,)), dma((2, 2)), dma((2, 2))],
        compiler_params=pltpu.CompilerParams(
            collective_id=0, has_side_effects=True, vmem_limit_bytes=56 * 2**20),
    )(activations, whitening, factor)


def solution(mesh):
    placed = (P("dp", "tensor"), P("tensor", None), P(("dp", "tensor"), None))
    return jax.shard_map(
        shards, mesh=mesh, in_specs=placed, out_specs=P(("dp", "tensor"), None), check_vma=False
    )
```

```python
import jax, jax.numpy as jnp
from jax import lax
from jax.sharding import PartitionSpec as P
from jax.experimental import pallas as pl
from jax.experimental.pallas import tpu as pltpu

F32, BF16 = jnp.float32, jnp.bfloat16
HI = lax.Precision.HIGHEST

def over_lanes(x, j):
    return jnp.broadcast_to(x[:, j:j + 1], (8, 128))

def over_sublanes(x, j):
    return jnp.broadcast_to(x[j:j + 1, :], (8, 128))

def tree(p):
    while len(p) > 1:
        p = [p[i] + p[i + 1] for i in range(0, len(p), 2)]
    return p[0]

def eliminate(rows, cols, first, s, lane, sub):
    base = first + 8 * s
    more = s + 1 < len(rows)
    inside = (lane >= base) & (lane < base + 8)
    panel = rows[s]
    if cols is None:
        cols = [over_lanes(panel, base + j) for j in range(8)]
    cols = list(cols)
    z = jnp.where(inside, jnp.where(lane - base == sub, 1.0, 0.0), panel)
    ahead = [over_lanes(panel, base + 8 + j) for j in range(8)] if more else []
    for m in range(4):
        a, b = 2 * m, 2 * m + 1
        ea, eb = cols[a], cols[b]
        g00, g10 = over_sublanes(ea, a), over_sublanes(ea, b)
        g01, g11 = over_sublanes(eb, a), over_sublanes(eb, b)
        r = 1.0 / (g00 * g11 - g01 * g10)
        q00, q01, q10, q11 = g11 * r, -(g01 * r), -(g10 * r), g00 * r
        fa = -(ea * q00 + eb * q10)
        fb = -(ea * q01 + eb * q11)
        fa = jnp.where(sub == a, q00, jnp.where(sub == b, q10, fa))
        fb = jnp.where(sub == a, q01, jnp.where(sub == b, q11, fb))
        pair = (sub == a) | (sub == b)

        def step(v):
            return (jnp.where(pair, 0.0, v) + fa * over_sublanes(v, a)) + fb * over_sublanes(v, b)

        for c in range(b + 1, 8):
            cols[c] = step(cols[c])
        z = step(z)
        ahead = [step(v) for v in ahead]
    following = None
    trow = [over_sublanes(z, j) for j in range(8)]
    for i in list(range(s + 1, len(rows))) + list(range(s)):
        v = rows[i]
        spread = [over_lanes(v, base + j) for j in range(8)]
        if i == s + 1:
            following = [
                over_lanes(v, base + 8 + j) - tree([spread[m] * over_sublanes(ahead[j], m) for m in range(8)])
                for j in range(8)]
        rows[i] = jnp.where(inside, 0.0, v) - tree([spread[j] * trow[j] for j in range(8)])
    rows[s] = z
    return following

def invert_block(rows, size, fill):
    lane = lax.broadcasted_iota(jnp.int32, (8, 128), 1)
    sub = lax.broadcasted_iota(jnp.int32, (8, 128), 0)
    each = size // 8
    groups = 128 // size
    zero = [jnp.zeros((8, 128), F32)]
    for g in range(groups):
        own = rows[each * g:each * g + each]
        cols = None
        for s in range(each):
            cols = eliminate(own, cols, size * g, s, lane, sub)
            fill()
        rows[each * g:each * g + each] = own
        inside = (lane >= size * g) & (lane < size * g + size)
        t = jnp.concatenate(zero * (each * g) + own + zero * (16 - each * g - each), axis=0)
        for o in [(g + e) % groups for e in range(1, groups)]:
            c = jnp.concatenate([jnp.where(inside, rows[i], 0.0) for i in range(each * o, each * o + each)], axis=0)
            u = jnp.dot(c, t, precision=HI, preferred_element_type=F32)
            for n in range(each):
                i = each * o + n
                rows[i] = jnp.where(inside, 0.0, rows[i]) - u[8 * n:8 * n + 8]
    return rows

TERMS = ((0, 0), (0, 1), (1, 0), (1, 1))
SIZE = 64
N = 1024
LAST = N - 128

def split(x):
    one = x.astype(BF16)
    rest = x - one.astype(F32)
    two = rest.astype(BF16)
    three = (rest - two.astype(F32)).astype(BF16)
    return one, two, three

def hadamard_block(f_ref, i, rows, j, cols):
    g = lax.dot_general(f_ref[:, i:i + rows], f_ref[:, j:j + cols], (((0,), (0,)), ((), ())), preferred_element_type=F32)
    row = lax.broadcasted_iota(jnp.int32, (rows, cols), 0) + i
    col = lax.broadcasted_iota(jnp.int32, (rows, cols), 1) + j
    return g * g + jnp.where(row == col, 0.1, 0.0)

def invert(f_ref, inv_ref, left, right, pivot, between):
    def run(todo, rate):
        def fill():
            for _ in range(rate):
                if todo:
                    todo.pop(0)()
        return fill

    def fill_rows(j):
        def go():
            inv_ref[128 * j:128 * j + 128, :] = hadamard_block(f_ref, 128 * j, 128, 0, N)
        return go

    d = hadamard_block(f_ref, 0, 128, 0, 128)
    todo = [fill_rows(j) for j in range(8)]
    first = invert_block([d[8 * i:8 * i + 8] for i in range(16)], SIZE, run(todo, 1))
    pivot[...] = jnp.concatenate(first, axis=0)

    def work(k0):
        p = pivot[...]
        row = lax.broadcasted_iota(jnp.int32, (N, 128), 0)
        col = lax.broadcasted_iota(jnp.int32, (128, 256), 1)
        own = (row >= k0) & (row < k0 + 128)
        pp = jnp.concatenate([p, p], axis=1)

        def panel(j):
            def go():
                cols = slice(256 * j, 256 * j + 256)
                t = jnp.dot(p, inv_ref[pl.ds(k0, 128), cols], precision=HI, preferred_element_type=F32)
                at = col + 256 * j
                t = jnp.where((at >= k0) & (at < k0 + 128), pp, t)
                inv_ref[pl.ds(k0, 128), cols] = t
                tt = split(t)
                for i, (a, b) in enumerate(TERMS):
                    right[128 * i:128 * i + 128, cols] = tt[b]
            return go

        def column():
            old = inv_ref[:, pl.ds(k0, 128)]
            cc = split(jnp.where(own, 0.0, old))
            for i, (a, b) in enumerate(TERMS):
                left[:, 128 * i:128 * i + 128] = cc[a]
            inv_ref[:, pl.ds(k0, 128)] = jnp.where(own, old, 0.0)

        def update(r, c):
            def go():
                rows, cols = slice(128 * r, 128 * r + 128), slice(512 * c, 512 * c + 512)
                inv_ref[rows, cols] -= jnp.dot(left[rows, :], right[:, cols], preferred_element_type=F32)
            return go

        return [column] + [panel(j) for j in range(4)] + [update(r, c) for r in range(8) for c in range(2)]

    def step(k, carry):
        between(k)
        k0 = pl.multiple_of(k * 128, 128)
        n0 = pl.multiple_of(k * 128 + 128, 128)
        p = pivot[...]
        tn = jnp.dot(p, inv_ref[pl.ds(k0, 128), pl.ds(n0, 128)], precision=HI, preferred_element_type=F32)
        d = inv_ref[pl.ds(n0, 128), pl.ds(n0, 128)] - jnp.dot(
            inv_ref[pl.ds(n0, 128), pl.ds(k0, 128)], tn, precision=HI, preferred_element_type=F32)
        todo = work(k0)
        nxt = invert_block([d[8 * i:8 * i + 8] for i in range(16)], SIZE, run(todo, 2))
        while todo:
            todo.pop(0)()
        pivot[...] = jnp.concatenate(nxt, axis=0)
        return carry

    lax.fori_loop(0, N // 128 - 1, step, 0)


MESH = pl.DeviceIdType.MESH
PARTS = ((0, 384, (0, 1, 2)), (384, 384, (1, 2, 0)), (768, 256, (2, 0, 1)))
STAGES = (3, 4, 5, 6, None)


def ring(i):
    return [i] + [jnp.where(i + s >= 4, i + s - 4, i + s) for s in (1, 2, 3)]


class Map:
    def __init__(self):
        dp, z = lax.axis_index("dp"), lax.axis_index("tensor")
        self.c = dp % 2
        self.at = (dp // 8, (dp // 2) % 4, z)
        self.rings = [ring(i) for i in self.at]
        self.partner = self.name(self.at, 1 - self.c)

    def name(self, at, core):
        return ((at[0] * 4 + at[1]) * 2 + core, at[2])

    def peer(self, axis, s):
        at = list(self.at)
        at[axis] = self.rings[axis][s]
        return self.name(at, self.c)

    def close(self):
        x, y, _ = self.at
        zs = self.rings[2]
        return [self.name((x, y, zs[s]), core) for core in (self.c, 1 - self.c) for s in range(4) if core is not self.c or s]

    def plane(self):
        xs, ys, _ = self.rings
        return [self.name((xs[a], ys[b], self.at[2]), self.c) for a in range(4) for b in range(4) if a + b]


def greet(m):
    barrier = pltpu.get_barrier_semaphore()
    for device in m.close() + m.plane():
        pl.semaphore_signal(barrier, inc=1, device_id=device, device_id_type=MESH)
    return barrier


def remote(src, dst, send, recv, device):
    return pltpu.make_async_remote_copy(
        src_ref=src, dst_ref=dst, send_sem=send, recv_sem=recv, device_id=device, device_id_type=MESH)


def all_of(ref, sem):
    return pltpu.make_async_copy(ref, ref, sem)


def whole_kernel(act_ref, wh_ref, f_ref, out_ref,
                 act, wh, part, far, near, f5, factor, inv, left, right, pivot, summed, squared, moment,
                 core_out, core_in, mine, in1, out2, in2, out3, in3, total, norm_out, norm_in,
                 act_sem, wh_sem, f_send, f_recv, l_send, l_recv, s_send, s_recv, n_send, n_recv,
                 pair_send, pair_recv, far_send, far_recv, near_send, near_recv):
    m = Map()
    c = m.c
    x, y, z = m.at
    barrier = greet(m)
    zs = m.rings[2]
    order = (zs[2], zs[1], zs[3], z)

    def load(r):
        rows = pl.ds(pl.multiple_of(order[r] * 512, 512), 512)
        return pltpu.make_async_copy(act_ref.at[rows, :], act.at[r], act_sem.at[r])

    load_wh = pltpu.make_async_copy(wh_ref, wh, wh_sem)
    load_wh.start()
    for r in range(4):
        load(r).start()
    f5[x, y, c, z] = f_ref[...]
    pl.semaphore_wait(barrier, 22)

    first, second = pl.ds(0, 512), pl.ds(512, 512)
    hops = [
        (f_ref, f5.at[x, y, c, z], 2, f5.at[0, 0, 0, pl.ds(0, 3)]),
        (f5.at[x, y, c, :, :, first], f5.at[x, y, c, :, :, first], 0, f5.at[pl.ds(0, 3), 0, 0, :, :, first]),
        (f5.at[x, y, c, :, :, second], f5.at[x, y, c, :, :, second], 1, f5.at[pl.ds(0, 3), 0, 0, :, :, first]),
    ]

    def hop_start(i):
        src, dst, axis, _ = hops[i]
        for s in (1, 2, 3):
            remote(src, dst, f_send.at[i], f_recv.at[i], m.peer(axis, s)).start()

    def hop_end(i, sems):
        all_of(hops[i][3], sems.at[i]).wait()

    def strip(half, s):
        if half == 0:
            return f5.at[:, m.rings[1][s], c, :, :, first]
        return f5.at[x, :, c, :, :, second] if s == 0 else f5.at[m.rings[0][s], :, c, :, :, second]

    def last_hop(half, s):
        return remote(strip(half, 0), strip(half, 0), l_send.at[half, s - 1], l_recv.at[half, s - 1], m.peer(1 - half, s))

    def pair(half, s):
        return remote(strip(half, s), strip(half, s), pair_send.at[0], pair_recv.at[0], m.partner)

    hop_start(0)

    up, down = m.peer(2, 1), m.peer(2, 3)
    far_up = remote(part.at[0, pl.ds(0, 256)], far.at[0], far_send.at[0], far_recv.at[0], up)
    far_down = remote(part.at[0, pl.ds(256, 256)], far.at[1], far_send.at[1], far_recv.at[1], down)

    def near_copy(slot, half):
        rows = pl.ds(256 * half, 256)
        return remote(part.at[1 + slot, rows], near.at[slot, rows], near_send.at[slot, half], near_recv.at[slot, half],
                      down if slot else up)

    load_wh.wait()
    for r in range(4):
        load(r).wait()
        if r == 0:
            hop_end(0, f_recv)
            hop_start(1)
            hop_start(2)

        def tile(i, carry, r=r):
            cols = pl.ds(pl.multiple_of(i * 256, 256), 256)
            part[r, :, cols] = jnp.dot(act[r], wh[:, cols], preferred_element_type=F32).astype(BF16)
            return carry

        def half_tile(i, carry, r=r):
            rows = pl.ds(pl.multiple_of((i // 4) * 256, 256), 256)
            cols = pl.ds(pl.multiple_of((i % 4) * 256, 256), 256)
            part[r, rows, cols] = jnp.dot(act[r, rows, :], wh[:, cols], preferred_element_type=F32).astype(BF16)
            return carry

        if r == 0:
            lax.fori_loop(0, 4, half_tile, 0)
            far_up.start()
            lax.fori_loop(4, 8, half_tile, 0)
            far_down.start()
        else:
            lax.fori_loop(0, 4, tile, 0)
        if r == 0:
            hop_end(1, f_recv)
            hop_end(2, f_recv)
            for s in (1, 2, 3):
                for half in (0, 1):
                    last_hop(half, s).start()
            for half in (0, 1):
                pair(half, 0).start()
        if r == 1:
            near_copy(0, 1).start()
        if r == 2:
            near_copy(1, 0).start()
            for s in (1, 3, 2):
                for half in (0, 1):
                    last_hop(half, s).wait_recv()
                    pair(half, 4 - s).start()

    def forward(copy_in, slot):
        begin = 256 * slot
        copy_in.wait_recv()

        def add(i, carry):
            here = pl.ds(pl.multiple_of(i * 32, 32), 32)
            rows = pl.ds(pl.multiple_of(begin + i * 32, 32), 32)
            part[1 + slot, rows, :] = (part[1 + slot, rows, :].astype(F32) + far[slot, here, :].astype(F32)).astype(BF16)
            return carry

        lax.fori_loop(0, 8, add, 0)
        near_copy(slot, slot).start()

    forward(far_up, 0)
    forward(far_down, 1)
    all_of(f5.at[:, :, 0], pair_recv.at[0]).wait()

    def flatten(i, carry):
        for e in range(2):
            for h in range(2):
                block = jnp.concatenate(
                    [f5[i // 4, i % 4, e, 2 * h].astype(F32), f5[i // 4, i % 4, e, 2 * h + 1].astype(F32)], axis=0)
                factor[pl.ds(pl.multiple_of(i * 64 + 32 * e + 16 * h, 16), 16), :] = block.astype(BF16)
        return carry

    lax.fori_loop(0, 16, flatten, 0)

    across = remote(core_out, core_in, pair_send.at[1], pair_recv.at[1], m.partner)

    def rows_of(i, core):
        return pl.ds(pl.multiple_of((i * 2 + core) * 32, 32), 32)

    def stage_moment():
        for slot in (0, 1):
            for half in (0, 1):
                near_copy(slot, half).wait_recv()

        def add(i, carry):
            rows = pl.ds(pl.multiple_of(i * 32, 32), 32)
            summed[rows, :] = (part[3, rows, :].astype(F32) + near[0, rows, :].astype(F32)
                               + near[1, rows, :].astype(F32)).astype(BF16)
            return carry

        lax.fori_loop(0, 16, add, 0)

        def project(i, carry):
            cols = pl.ds(pl.multiple_of(i * 256, 256), 256)
            p = jnp.dot(summed[...], factor[:, cols], preferred_element_type=F32)
            squared[:, cols] = (p * p).astype(BF16)
            return carry

        lax.fori_loop(0, 4, project, 0)

        def moments(i, carry):
            rows = pl.ds(pl.multiple_of(i * 256, 256), 256)
            moment[rows, :] = lax.dot_general(
                summed[:, rows], squared[...], (((0,), (0,)), ((), ())), preferred_element_type=F32)
            return carry

        lax.fori_loop(0, 4, moments, 0)

        def cast(i, carry):
            core_out[i] = moment[rows_of(i, 1 - c), :].reshape(4, 8, N).astype(BF16)
            return carry

        lax.fori_loop(0, 16, cast, 0)
        across.start()

    def pick(ref, fixed, cols):
        index = [fixed.get(axis, slice(None)) for axis in range(3)]
        return ref.at[(*index, slice(None), pl.ds(cols[0], cols[1]))]

    def send1(p, s):
        lo, width, (a, b, e) = PARTS[p]
        src = pick(mine, {a: m.rings[a][s]}, (lo, width))
        return remote(src, in1.at[s - 1, :, :, :, pl.ds(lo, width)], s_send.at[0, p], s_recv.at[0, p], m.peer(a, s))

    def send2(p, s):
        lo, width, (a, b, e) = PARTS[p]
        src = out2.at[m.rings[b][s], :, :, pl.ds(lo, width)]
        return remote(src, in2.at[s - 1, :, :, pl.ds(lo, width)], s_send.at[1, p], s_recv.at[1, p], m.peer(b, s))

    def send3(p, s):
        lo, width, (a, b, e) = PARTS[p]
        src = out3.at[m.rings[e][s], :, pl.ds(lo, width)]
        return remote(src, in3.at[s - 1, :, pl.ds(lo, width)], s_send.at[2, p], s_recv.at[2, p], m.peer(e, s))

    def landed(level, p, sems):
        lo, width, _ = PARTS[p]
        ref = (in1.at[:, :, :, :, pl.ds(lo, width)], in2.at[:, :, :, pl.ds(lo, width)], in3.at[:, :, pl.ds(lo, width)])[level]
        all_of(ref, sems.at[level, p]).wait()

    def stage_cores():
        across.wait_recv()

        def add(i, carry):
            block = moment[rows_of(i, c), :].reshape(4, 8, N) + core_in[i].astype(F32)
            moment[rows_of(i, c), :] = block.reshape(32, N)
            mine[i // 4, i % 4] = block.astype(BF16)
            return carry

        lax.fori_loop(0, 16, add, 0)
        for s in (1, 2, 3):
            for p in range(3):
                send1(p, s).start()

    def gather_sum(row, many, cols, blocks):
        rows = pl.ds(pl.multiple_of(row, 8), 8 * many)
        t = moment[rows, cols]
        for block in blocks:
            t = t + block.astype(F32).reshape(8 * many, cols.size)
        moment[rows, cols] = t
        return t.astype(BF16).reshape(many, 8, cols.size)

    def row_at(ix, iy, iz):
        return (((ix * 4 + iy) * 2 + c) * 4 + iz) * 8

    def stage_one():
        spans = [pl.ds(lo, width) for lo, width, _ in PARTS]
        landed(0, 0, s_recv)

        def add_x(i, carry):
            out2[i, :, :, spans[0]] = gather_sum(
                row_at(x, i, 0), 4, spans[0], [in1[s, i, :, :, spans[0]] for s in range(3)])
            return carry

        lax.fori_loop(0, 4, add_x, 0)
        for s in (1, 2, 3):
            send2(0, s).start()
        landed(0, 1, s_recv)

        def add_y(i, carry):
            out2[:, i, :, spans[1]] = gather_sum(
                row_at(i, y, 0), 4, spans[1], [in1[s, i, :, :, spans[1]] for s in range(3)])
            return carry

        lax.fori_loop(0, 4, add_y, 0)
        for s in (1, 2, 3):
            send2(1, s).start()
        landed(0, 2, s_recv)

        def add_z(i, carry):
            for j in range(4):
                out2[i, pl.ds(j, 1), :, spans[2]] = gather_sum(
                    row_at(i, j, z), 1, spans[2], [in1[s, i, j, :, spans[2]] for s in range(3)])
            return carry

        lax.fori_loop(0, 4, add_z, 0)
        for s in (1, 2, 3):
            send2(2, s).start()

    def stage_two():
        spans = [pl.ds(lo, width) for lo, width, _ in PARTS]
        landed(1, 0, s_recv)
        out3[:, :, spans[0]] = gather_sum(row_at(x, y, 0), 4, spans[0], [in2[s, :, :, spans[0]] for s in range(3)])
        for s in (1, 2, 3):
            send3(0, s).start()
        for p in (1, 2):
            landed(1, p, s_recv)
            for i in range(4):
                row = row_at(i, y, z) if p == 1 else row_at(x, i, z)
                out3[pl.ds(i, 1), :, spans[p]] = gather_sum(row, 1, spans[p], [in2[s, i, :, spans[p]] for s in range(3)])
            for s in (1, 2, 3):
                send3(p, s).start()

    def stage_three():
        own = pl.multiple_of((((x * 4 + y) * 2 + c) * 4 + z) * 8, 8)
        for p in range(3):
            lo, width, _ = PARTS[p]
            cols = pl.ds(lo, width)
            landed(2, p, s_recv)
            t = moment[pl.ds(own, 8), cols]
            for s in range(3):
                t = t + in3[s, :, cols].astype(F32)
            total[:, cols] = t

    stages = (stage_moment, stage_cores, stage_one, stage_two, stage_three)

    def between(k):
        for stage, when in zip(stages, STAGES):
            if when is not None:
                pl.when(k == when)(stage)

    invert(factor, inv, left, right, pivot, between)
    for stage, when in zip(stages, STAGES):
        if when is None:
            stage()
    moved = jnp.where(lax.broadcasted_iota(jnp.int32, (8, N), 1) < LAST, total[...], 0.0)
    partly = jnp.dot(moved, inv[...], precision=HI, preferred_element_type=F32)
    corner = jnp.dot(total[:, LAST:] - partly[:, LAST:], pivot[...], precision=HI, preferred_element_type=F32)
    others = partly[:, :LAST] + jnp.dot(corner, inv[LAST:, :LAST], precision=HI, preferred_element_type=F32)
    updated = jnp.concatenate([others, corner], axis=1)

    squares = jnp.sum(updated * updated, axis=0, keepdims=True)
    for j in range(8):
        norm_out[0, j:j + 1, :] = squares[:, 128 * j:128 * j + 128]
    close, plane = m.close(), m.plane()
    for i, device in enumerate(close):
        remote(norm_out.at[0], norm_in.at[i], n_send.at[0], n_recv.at[0], device).start()
    all_of(norm_in.at[pl.ds(0, 7)], n_recv.at[0]).wait()
    norm = tree([norm_out[0]] + [norm_in[i] for i in range(7)])
    norm_out[1] = norm
    for i, device in enumerate(plane):
        remote(norm_out.at[1], norm_in.at[7 + i], n_send.at[1], n_recv.at[1], device).start()
    all_of(norm_in.at[pl.ds(7, 15)], n_recv.at[1]).wait()
    norm = tree([norm] + [norm_in[7 + i] for i in range(15)])
    scale = jnp.sqrt(norm * (1.0 / N) + 1e-6)
    for j in range(8):
        cols = slice(128 * j, 128 * j + 128)
        out_ref[:, cols] = updated[:, cols] / scale[j:j + 1, :]

    for i in range(3):
        hop_end(i, f_send)
    for s in (1, 2, 3):
        for half in (0, 1):
            last_hop(half, s).wait_send()
    for level in range(3):
        for p in range(3):
            landed(level, p, s_send)
    all_of(norm_in.at[pl.ds(0, 7)], n_send.at[0]).wait()
    all_of(norm_in.at[pl.ds(7, 15)], n_send.at[1]).wait()
    all_of(f5.at[:, :, 0], pair_send.at[0]).wait()
    for slot in (0, 1):
        for half in (0, 1):
            near_copy(slot, half).wait_send()
    for copy in (across, far_up, far_down):
        copy.wait_send()


def shards(activations, whitening, factor):
    terms = 128 * len(TERMS)
    dma = pltpu.SemaphoreType.DMA
    return pl.pallas_call(
        whole_kernel,
        out_shape=jax.ShapeDtypeStruct((8, N), F32),
        in_specs=[pl.BlockSpec(memory_space=pl.ANY)] * 2 + [pl.BlockSpec(memory_space=pltpu.VMEM)],
        out_specs=pl.BlockSpec(memory_space=pltpu.VMEM),
        scratch_shapes=[
            pltpu.VMEM((4, 512, 2048), BF16), pltpu.VMEM((2048, N), BF16), pltpu.VMEM((4, 512, N), BF16),
            pltpu.VMEM((2, 256, N), BF16), pltpu.VMEM((2, 512, N), BF16),
            pltpu.VMEM((4, 4, 2, 4, 8, N), BF16), pltpu.VMEM((N, N), BF16), pltpu.VMEM((N, N), F32),
            pltpu.VMEM((N, terms), BF16), pltpu.VMEM((terms, N), BF16), pltpu.VMEM((128, 128), F32),
            pltpu.VMEM((512, N), BF16), pltpu.VMEM((512, N), BF16), pltpu.VMEM((N, N), F32),
            pltpu.VMEM((16, 4, 8, N), BF16), pltpu.VMEM((16, 4, 8, N), BF16), pltpu.VMEM((4, 4, 4, 8, N), BF16),
            pltpu.VMEM((3, 4, 4, 8, N), BF16), pltpu.VMEM((4, 4, 8, N), BF16), pltpu.VMEM((3, 4, 8, N), BF16),
            pltpu.VMEM((4, 8, N), BF16), pltpu.VMEM((3, 8, N), BF16), pltpu.VMEM((8, N), F32),
            pltpu.VMEM((2, 8, 128), F32), pltpu.VMEM((22, 8, 128), F32),
            dma((4,)), dma, dma((3,)), dma((3,)), dma((2, 3)), dma((2, 3)), dma((3, 3)), dma((3, 3)), dma((2,)), dma((2,)),
            dma((2,)), dma((2,)), dma((2,)), dma((2,)), dma((2, 2)), dma((2, 2))],
        compiler_params=pltpu.CompilerParams(
            collective_id=0, has_side_effects=True, vmem_limit_bytes=56 * 2**20),
    )(activations, whitening, factor)


def solution(mesh):
    placed = (P("dp", "tensor"), P("tensor", None), P(("dp", "tensor"), None))
    return jax.shard_map(
        shards, mesh=mesh, in_specs=placed, out_specs=P(("dp", "tensor"), None), check_vma=False
    )
```

```python
import jax, jax.numpy as jnp
from jax import lax
from jax.sharding import PartitionSpec as P
from jax.experimental import pallas as pl
from jax.experimental.pallas import tpu as pltpu

F32, BF16 = jnp.float32, jnp.bfloat16
HI = lax.Precision.HIGHEST

def over_lanes(x, j):
    return jnp.broadcast_to(x[:, j:j + 1], (8, 128))

def over_sublanes(x, j):
    return jnp.broadcast_to(x[j:j + 1, :], (8, 128))

def tree(p):
    while len(p) > 1:
        p = [p[i] + p[i + 1] for i in range(0, len(p), 2)]
    return p[0]

def eliminate(rows, cols, first, s, lane, sub):
    base = first + 8 * s
    more = s + 1 < len(rows)
    inside = (lane >= base) & (lane < base + 8)
    panel = rows[s]
    if cols is None:
        cols = [over_lanes(panel, base + j) for j in range(8)]
    cols = list(cols)
    z = jnp.where(inside, jnp.where(lane - base == sub, 1.0, 0.0), panel)
    ahead = [over_lanes(panel, base + 8 + j) for j in range(8)] if more else []
    for m in range(4):
        a, b = 2 * m, 2 * m + 1
        ea, eb = cols[a], cols[b]
        g00, g10 = over_sublanes(ea, a), over_sublanes(ea, b)
        g01, g11 = over_sublanes(eb, a), over_sublanes(eb, b)
        r = 1.0 / (g00 * g11 - g01 * g10)
        q00, q01, q10, q11 = g11 * r, -(g01 * r), -(g10 * r), g00 * r
        fa = -(ea * q00 + eb * q10)
        fb = -(ea * q01 + eb * q11)
        fa = jnp.where(sub == a, q00, jnp.where(sub == b, q10, fa))
        fb = jnp.where(sub == a, q01, jnp.where(sub == b, q11, fb))
        pair = (sub == a) | (sub == b)

        def step(v):
            return (jnp.where(pair, 0.0, v) + fa * over_sublanes(v, a)) + fb * over_sublanes(v, b)

        for c in range(b + 1, 8):
            cols[c] = step(cols[c])
        z = step(z)
        ahead = [step(v) for v in ahead]
    following = None
    trow = [over_sublanes(z, j) for j in range(8)]
    for i in list(range(s + 1, len(rows))) + list(range(s)):
        v = rows[i]
        spread = [over_lanes(v, base + j) for j in range(8)]
        if i == s + 1:
            following = [
                over_lanes(v, base + 8 + j) - tree([spread[m] * over_sublanes(ahead[j], m) for m in range(8)])
                for j in range(8)]
        rows[i] = jnp.where(inside, 0.0, v) - tree([spread[j] * trow[j] for j in range(8)])
    rows[s] = z
    return following

def product(a, b):
    a1 = a.astype(BF16)
    a2 = (a - a1.astype(F32)).astype(BF16)
    b1 = b.astype(BF16)
    b2 = (b - b1.astype(F32)).astype(BF16)
    left = jnp.concatenate([a1, a1, a2, a2], axis=1)
    right = jnp.concatenate([b1, b2, b1, b2], axis=0)
    return jnp.dot(left, right, preferred_element_type=F32)

def invert_block(rows, size, fill):
    lane = lax.broadcasted_iota(jnp.int32, (8, 128), 1)
    sub = lax.broadcasted_iota(jnp.int32, (8, 128), 0)
    each = size // 8
    groups = 128 // size
    zero = [jnp.zeros((8, 128), F32)]
    for g in range(groups):
        own = rows[each * g:each * g + each]
        cols = None
        for s in range(each):
            cols = eliminate(own, cols, size * g, s, lane, sub)
            fill()
        rows[each * g:each * g + each] = own
        inside = (lane >= size * g) & (lane < size * g + size)
        t = jnp.concatenate(zero * (each * g) + own + zero * (16 - each * g - each), axis=0)
        for o in [(g + e) % groups for e in range(1, groups)]:
            c = jnp.concatenate([jnp.where(inside, rows[i], 0.0) for i in range(each * o, each * o + each)], axis=0)
            u = product(c, t)
            for n in range(each):
                i = each * o + n
                rows[i] = jnp.where(inside, 0.0, rows[i]) - u[8 * n:8 * n + 8]
    return rows

TERMS = ((0, 0), (0, 1), (1, 0), (1, 1))
SIZE = 64
N = 1024
LAST = N - 128

def split(x):
    one = x.astype(BF16)
    rest = x - one.astype(F32)
    two = rest.astype(BF16)
    three = (rest - two.astype(F32)).astype(BF16)
    return one, two, three

def hadamard_block(f_ref, i, rows, j, cols):
    g = lax.dot_general(f_ref[:, i:i + rows], f_ref[:, j:j + cols], (((0,), (0,)), ((), ())), preferred_element_type=F32)
    row = lax.broadcasted_iota(jnp.int32, (rows, cols), 0) + i
    col = lax.broadcasted_iota(jnp.int32, (rows, cols), 1) + j
    return g * g + jnp.where(row == col, 0.1, 0.0)

def invert(f_ref, inv_ref, left, right, pivot, between):
    def run(todo, rate):
        def fill():
            for _ in range(rate):
                if todo:
                    todo.pop(0)()
        return fill

    def fill_rows(j):
        def go():
            inv_ref[128 * j:128 * j + 128, :] = hadamard_block(f_ref, 128 * j, 128, 0, N)
        return go

    d = hadamard_block(f_ref, 0, 128, 0, 128)
    todo = [fill_rows(j) for j in range(8)]
    first = invert_block([d[8 * i:8 * i + 8] for i in range(16)], SIZE, run(todo, 1))
    pivot[...] = jnp.concatenate(first, axis=0)

    def work(k0):
        p = pivot[...]
        row = lax.broadcasted_iota(jnp.int32, (N, 128), 0)
        col = lax.broadcasted_iota(jnp.int32, (128, 256), 1)
        own = (row >= k0) & (row < k0 + 128)
        pp = jnp.concatenate([p, p], axis=1)

        def panel(j):
            def go():
                cols = slice(256 * j, 256 * j + 256)
                t = product(p, inv_ref[pl.ds(k0, 128), cols])
                at = col + 256 * j
                t = jnp.where((at >= k0) & (at < k0 + 128), pp, t)
                inv_ref[pl.ds(k0, 128), cols] = t
                tt = split(t)
                for i, (a, b) in enumerate(TERMS):
                    right[128 * i:128 * i + 128, cols] = tt[b]
            return go

        def column():
            old = inv_ref[:, pl.ds(k0, 128)]
            cc = split(jnp.where(own, 0.0, old))
            for i, (a, b) in enumerate(TERMS):
                left[:, 128 * i:128 * i + 128] = cc[a]
            inv_ref[:, pl.ds(k0, 128)] = jnp.where(own, old, 0.0)

        def update(r, c):
            def go():
                rows, cols = slice(128 * r, 128 * r + 128), slice(512 * c, 512 * c + 512)
                inv_ref[rows, cols] -= jnp.dot(left[rows, :], right[:, cols], preferred_element_type=F32)
            return go

        return [column] + [panel(j) for j in range(4)] + [update(r, c) for r in range(8) for c in range(2)]

    def step(k, carry):
        between(k)
        k0 = pl.multiple_of(k * 128, 128)
        n0 = pl.multiple_of(k * 128 + 128, 128)
        p = pivot[...]
        tn = product(p, inv_ref[pl.ds(k0, 128), pl.ds(n0, 128)])
        d = inv_ref[pl.ds(n0, 128), pl.ds(n0, 128)] - product(
            inv_ref[pl.ds(n0, 128), pl.ds(k0, 128)], tn)
        todo = work(k0)
        nxt = invert_block([d[8 * i:8 * i + 8] for i in range(16)], SIZE, run(todo, 2))
        while todo:
            todo.pop(0)()
        pivot[...] = jnp.concatenate(nxt, axis=0)
        return carry

    lax.fori_loop(0, N // 128 - 1, step, 0)


MESH = pl.DeviceIdType.MESH
PARTS = ((0, 384, (0, 1, 2)), (384, 384, (1, 2, 0)), (768, 256, (2, 0, 1)))
STAGES = (3, 4, 5, 6, None)


def ring(i):
    return [i] + [jnp.where(i + s >= 4, i + s - 4, i + s) for s in (1, 2, 3)]


class Map:
    def __init__(self):
        dp, z = lax.axis_index("dp"), lax.axis_index("tensor")
        self.c = dp % 2
        self.at = (dp // 8, (dp // 2) % 4, z)
        self.rings = [ring(i) for i in self.at]
        self.partner = self.name(self.at, 1 - self.c)

    def name(self, at, core):
        return ((at[0] * 4 + at[1]) * 2 + core, at[2])

    def peer(self, axis, s):
        at = list(self.at)
        at[axis] = self.rings[axis][s]
        return self.name(at, self.c)

    def close(self):
        x, y, _ = self.at
        zs = self.rings[2]
        return [self.name((x, y, zs[s]), core) for core in (self.c, 1 - self.c) for s in range(4) if core is not self.c or s]

    def plane(self):
        xs, ys, _ = self.rings
        return [self.name((xs[a], ys[b], self.at[2]), self.c) for a in range(4) for b in range(4) if a + b]


def greet(m):
    barrier = pltpu.get_barrier_semaphore()
    for device in m.close() + m.plane():
        pl.semaphore_signal(barrier, inc=1, device_id=device, device_id_type=MESH)
    return barrier


def remote(src, dst, send, recv, device):
    return pltpu.make_async_remote_copy(
        src_ref=src, dst_ref=dst, send_sem=send, recv_sem=recv, device_id=device, device_id_type=MESH)


def all_of(ref, sem):
    return pltpu.make_async_copy(ref, ref, sem)


def whole_kernel(act_ref, wh_ref, f_ref, out_ref,
                 act, wh, part, far, near, f5, factor, inv, left, right, pivot, summed, squared, moment,
                 core_out, core_in, mine, in1, out2, in2, out3, in3, total, norm_out, norm_in,
                 act_sem, wh_sem, f_send, f_recv, l_send, l_recv, s_send, s_recv, n_send, n_recv,
                 pair_send, pair_recv, far_send, far_recv, near_send, near_recv):
    m = Map()
    c = m.c
    x, y, z = m.at
    barrier = greet(m)
    zs = m.rings[2]
    order = (zs[2], zs[1], zs[3], z)

    def load(r):
        rows = pl.ds(pl.multiple_of(order[r] * 512, 512), 512)
        return pltpu.make_async_copy(act_ref.at[rows, :], act.at[r], act_sem.at[r])

    load_wh = pltpu.make_async_copy(wh_ref, wh, wh_sem)
    load_wh.start()
    for r in range(4):
        load(r).start()
    f5[x, y, c, z] = f_ref[...]
    pl.semaphore_wait(barrier, 22)

    first, second = pl.ds(0, 512), pl.ds(512, 512)
    hops = [
        (f_ref, f5.at[x, y, c, z], 2, f5.at[0, 0, 0, pl.ds(0, 3)]),
        (f5.at[x, y, c, :, :, first], f5.at[x, y, c, :, :, first], 0, f5.at[pl.ds(0, 3), 0, 0, :, :, first]),
        (f5.at[x, y, c, :, :, second], f5.at[x, y, c, :, :, second], 1, f5.at[pl.ds(0, 3), 0, 0, :, :, first]),
    ]

    def hop_start(i):
        src, dst, axis, _ = hops[i]
        for s in (2, 1, 3):
            remote(src, dst, f_send.at[i], f_recv.at[i], m.peer(axis, s)).start()

    def hop_end(i, sems):
        all_of(hops[i][3], sems.at[i]).wait()

    def strip(half, s):
        if half == 0:
            return f5.at[:, m.rings[1][s], c, :, :, first]
        return f5.at[x, :, c, :, :, second] if s == 0 else f5.at[m.rings[0][s], :, c, :, :, second]

    def last_hop(half, s):
        return remote(strip(half, 0), strip(half, 0), l_send.at[half, s - 1], l_recv.at[half, s - 1], m.peer(1 - half, s))

    def pair(half, s):
        return remote(strip(half, s), strip(half, s), pair_send.at[0], pair_recv.at[0], m.partner)

    hop_start(0)

    up, down = m.peer(2, 1), m.peer(2, 3)
    far_up = remote(part.at[0, pl.ds(0, 256)], far.at[0], far_send.at[0], far_recv.at[0], up)
    far_down = remote(part.at[0, pl.ds(256, 256)], far.at[1], far_send.at[1], far_recv.at[1], down)

    def near_copy(slot, half):
        rows = pl.ds(256 * half, 256)
        return remote(part.at[1 + slot, rows], near.at[slot, rows], near_send.at[slot, half], near_recv.at[slot, half],
                      down if slot else up)

    load_wh.wait()
    for r in range(4):
        load(r).wait()

        def tile(i, carry, r=r):
            cols = pl.ds(pl.multiple_of(i * 256, 256), 256)
            part[r, :, cols] = jnp.dot(act[r], wh[:, cols], preferred_element_type=F32).astype(BF16)
            return carry

        def half_tile(i, carry, r=r):
            rows = pl.ds(pl.multiple_of((i // 4) * 256, 256), 256)
            cols = pl.ds(pl.multiple_of((i % 4) * 256, 256), 256)
            part[r, rows, cols] = jnp.dot(act[r, rows, :], wh[:, cols], preferred_element_type=F32).astype(BF16)
            return carry

        if r == 0:
            lax.fori_loop(0, 4, half_tile, 0)
            far_up.start()
            lax.fori_loop(4, 8, half_tile, 0)
            far_down.start()
        else:
            lax.fori_loop(0, 4, tile, 0)
        if r == 0:
            hop_end(0, f_recv)
            hop_start(1)
            hop_start(2)
        if r == 1:
            hop_end(1, f_recv)
            hop_end(2, f_recv)
            for s in (2, 1, 3):
                for half in (0, 1):
                    last_hop(half, s).start()
            for half in (0, 1):
                pair(half, 0).start()
            near_copy(0, 1).start()
        if r == 2:
            near_copy(1, 0).start()
        if r == 3:
            for s in (1, 3, 2):
                for half in (0, 1):
                    last_hop(half, s).wait_recv()
                    pair(half, 4 - s).start()

    def forward(copy_in, slot):
        begin = 256 * slot
        copy_in.wait_recv()

        def add(i, carry):
            here = pl.ds(pl.multiple_of(i * 32, 32), 32)
            rows = pl.ds(pl.multiple_of(begin + i * 32, 32), 32)
            part[1 + slot, rows, :] = (part[1 + slot, rows, :].astype(F32) + far[slot, here, :].astype(F32)).astype(BF16)
            return carry

        lax.fori_loop(0, 8, add, 0)
        near_copy(slot, slot).start()

    forward(far_up, 0)
    forward(far_down, 1)
    all_of(f5.at[:, :, 0], pair_recv.at[0]).wait()

    def flatten(i, carry):
        for e in range(2):
            for h in range(2):
                block = jnp.concatenate(
                    [f5[i // 4, i % 4, e, 2 * h].astype(F32), f5[i // 4, i % 4, e, 2 * h + 1].astype(F32)], axis=0)
                factor[pl.ds(pl.multiple_of(i * 64 + 32 * e + 16 * h, 16), 16), :] = block.astype(BF16)
        return carry

    lax.fori_loop(0, 16, flatten, 0)

    across = remote(core_out, core_in, pair_send.at[1], pair_recv.at[1], m.partner)

    def rows_of(i, core):
        return pl.ds(pl.multiple_of((i * 2 + core) * 32, 32), 32)

    def stage_moment():
        for slot in (0, 1):
            for half in (0, 1):
                near_copy(slot, half).wait_recv()

        def add(i, carry):
            rows = pl.ds(pl.multiple_of(i * 32, 32), 32)
            summed[rows, :] = (part[3, rows, :].astype(F32) + near[0, rows, :].astype(F32)
                               + near[1, rows, :].astype(F32)).astype(BF16)
            return carry

        lax.fori_loop(0, 16, add, 0)

        def project(i, carry):
            cols = pl.ds(pl.multiple_of(i * 256, 256), 256)
            p = jnp.dot(summed[...], factor[:, cols], preferred_element_type=F32)
            squared[:, cols] = (p * p).astype(BF16)
            return carry

        lax.fori_loop(0, 4, project, 0)

        def moments(i, carry):
            rows = pl.ds(pl.multiple_of(i * 256, 256), 256)
            moment[rows, :] = lax.dot_general(
                summed[:, rows], squared[...], (((0,), (0,)), ((), ())), preferred_element_type=F32)
            return carry

        lax.fori_loop(0, 4, moments, 0)

        def cast(i, carry):
            core_out[i] = moment[rows_of(i, 1 - c), :].reshape(4, 8, N).astype(BF16)
            return carry

        lax.fori_loop(0, 16, cast, 0)
        across.start()

    def pick(ref, fixed, cols):
        index = [fixed.get(axis, slice(None)) for axis in range(3)]
        return ref.at[(*index, slice(None), pl.ds(cols[0], cols[1]))]

    def send1(p, s):
        lo, width, (a, b, e) = PARTS[p]
        src = pick(mine, {a: m.rings[a][s]}, (lo, width))
        return remote(src, in1.at[s - 1, :, :, :, pl.ds(lo, width)], s_send.at[0, p], s_recv.at[0, p], m.peer(a, s))

    def send2(p, s):
        lo, width, (a, b, e) = PARTS[p]
        src = out2.at[m.rings[b][s], :, :, pl.ds(lo, width)]
        return remote(src, in2.at[s - 1, :, :, pl.ds(lo, width)], s_send.at[1, p], s_recv.at[1, p], m.peer(b, s))

    def send3(p, s):
        lo, width, (a, b, e) = PARTS[p]
        src = out3.at[m.rings[e][s], :, pl.ds(lo, width)]
        return remote(src, in3.at[s - 1, :, pl.ds(lo, width)], s_send.at[2, p], s_recv.at[2, p], m.peer(e, s))

    def landed(level, p, sems):
        lo, width, _ = PARTS[p]
        ref = (in1.at[:, :, :, :, pl.ds(lo, width)], in2.at[:, :, :, pl.ds(lo, width)], in3.at[:, :, pl.ds(lo, width)])[level]
        all_of(ref, sems.at[level, p]).wait()

    def stage_cores():
        across.wait_recv()

        def add(i, carry):
            block = moment[rows_of(i, c), :].reshape(4, 8, N) + core_in[i].astype(F32)
            moment[rows_of(i, c), :] = block.reshape(32, N)
            mine[i // 4, i % 4] = block.astype(BF16)
            return carry

        lax.fori_loop(0, 16, add, 0)
        for s in (2, 1, 3):
            for p in range(3):
                send1(p, s).start()

    def gather_sum(row, many, cols, blocks):
        rows = pl.ds(pl.multiple_of(row, 8), 8 * many)
        t = moment[rows, cols]
        for block in blocks:
            t = t + block.astype(F32).reshape(8 * many, cols.size)
        moment[rows, cols] = t
        return t.astype(BF16).reshape(many, 8, cols.size)

    def row_at(ix, iy, iz):
        return (((ix * 4 + iy) * 2 + c) * 4 + iz) * 8

    def stage_one():
        spans = [pl.ds(lo, width) for lo, width, _ in PARTS]
        landed(0, 0, s_recv)

        def add_x(i, carry):
            out2[i, :, :, spans[0]] = gather_sum(
                row_at(x, i, 0), 4, spans[0], [in1[s, i, :, :, spans[0]] for s in range(3)])
            return carry

        lax.fori_loop(0, 4, add_x, 0)
        for s in (2, 1, 3):
            send2(0, s).start()
        landed(0, 1, s_recv)

        def add_y(i, carry):
            out2[:, i, :, spans[1]] = gather_sum(
                row_at(i, y, 0), 4, spans[1], [in1[s, i, :, :, spans[1]] for s in range(3)])
            return carry

        lax.fori_loop(0, 4, add_y, 0)
        for s in (2, 1, 3):
            send2(1, s).start()
        landed(0, 2, s_recv)

        def add_z(i, carry):
            for j in range(4):
                out2[i, pl.ds(j, 1), :, spans[2]] = gather_sum(
                    row_at(i, j, z), 1, spans[2], [in1[s, i, j, :, spans[2]] for s in range(3)])
            return carry

        lax.fori_loop(0, 4, add_z, 0)
        for s in (2, 1, 3):
            send2(2, s).start()

    def stage_two():
        spans = [pl.ds(lo, width) for lo, width, _ in PARTS]
        landed(1, 0, s_recv)
        out3[:, :, spans[0]] = gather_sum(row_at(x, y, 0), 4, spans[0], [in2[s, :, :, spans[0]] for s in range(3)])
        for s in (2, 1, 3):
            send3(0, s).start()
        for p in (1, 2):
            landed(1, p, s_recv)
            for i in range(4):
                row = row_at(i, y, z) if p == 1 else row_at(x, i, z)
                out3[pl.ds(i, 1), :, spans[p]] = gather_sum(row, 1, spans[p], [in2[s, i, :, spans[p]] for s in range(3)])
            for s in (2, 1, 3):
                send3(p, s).start()

    def stage_three():
        own = pl.multiple_of((((x * 4 + y) * 2 + c) * 4 + z) * 8, 8)
        for p in range(3):
            lo, width, _ = PARTS[p]
            cols = pl.ds(lo, width)
            landed(2, p, s_recv)
            t = moment[pl.ds(own, 8), cols]
            for s in range(3):
                t = t + in3[s, :, cols].astype(F32)
            total[:, cols] = t

    stages = (stage_moment, stage_cores, stage_one, stage_two, stage_three)

    def between(k):
        for stage, when in zip(stages, STAGES):
            if when is not None:
                pl.when(k == when)(stage)

    invert(factor, inv, left, right, pivot, between)
    for stage, when in zip(stages, STAGES):
        if when is None:
            stage()
    moved = jnp.where(lax.broadcasted_iota(jnp.int32, (8, N), 1) < LAST, total[...], 0.0)
    stacked = jnp.concatenate([piece.astype(F32) for piece in split(moved)], axis=0).astype(BF16)
    partly = jnp.zeros((8, N), F32)
    for piece in split(inv[...])[:2]:
        products = jnp.dot(stacked, piece, preferred_element_type=F32)
        partly = partly + ((products[16:24] + products[8:16]) + products[0:8])
    corner = jnp.dot(total[:, LAST:] - partly[:, LAST:], pivot[...], precision=HI, preferred_element_type=F32)
    others = partly[:, :LAST] + jnp.dot(corner, inv[LAST:, :LAST], precision=HI, preferred_element_type=F32)
    updated = jnp.concatenate([others, corner], axis=1)

    squares = jnp.sum(updated * updated, axis=0, keepdims=True)
    for j in range(8):
        norm_out[0, j:j + 1, :] = squares[:, 128 * j:128 * j + 128]
    close, plane = m.close(), m.plane()
    for i, device in enumerate(close):
        remote(norm_out.at[0], norm_in.at[i], n_send.at[0], n_recv.at[0], device).start()
    all_of(norm_in.at[pl.ds(0, 7)], n_recv.at[0]).wait()
    norm = tree([norm_out[0]] + [norm_in[i] for i in range(7)])
    norm_out[1] = norm
    for i, device in enumerate(plane):
        remote(norm_out.at[1], norm_in.at[7 + i], n_send.at[1], n_recv.at[1], device).start()
    all_of(norm_in.at[pl.ds(7, 15)], n_recv.at[1]).wait()
    norm = tree([norm] + [norm_in[7 + i] for i in range(15)])
    scale = jnp.sqrt(norm * (1.0 / N) + 1e-6)
    for j in range(8):
        cols = slice(128 * j, 128 * j + 128)
        out_ref[:, cols] = updated[:, cols] / scale[j:j + 1, :]

    for i in range(3):
        hop_end(i, f_send)
    for s in (2, 1, 3):
        for half in (0, 1):
            last_hop(half, s).wait_send()
    for level in range(3):
        for p in range(3):
            landed(level, p, s_send)
    all_of(norm_in.at[pl.ds(0, 7)], n_send.at[0]).wait()
    all_of(norm_in.at[pl.ds(7, 15)], n_send.at[1]).wait()
    all_of(f5.at[:, :, 0], pair_send.at[0]).wait()
    for slot in (0, 1):
        for half in (0, 1):
            near_copy(slot, half).wait_send()
    for copy in (across, far_up, far_down):
        copy.wait_send()


def shards(activations, whitening, factor):
    terms = 128 * len(TERMS)
    dma = pltpu.SemaphoreType.DMA
    return pl.pallas_call(
        whole_kernel,
        out_shape=jax.ShapeDtypeStruct((8, N), F32),
        in_specs=[pl.BlockSpec(memory_space=pl.ANY)] * 2 + [pl.BlockSpec(memory_space=pltpu.VMEM)],
        out_specs=pl.BlockSpec(memory_space=pltpu.VMEM),
        scratch_shapes=[
            pltpu.VMEM((4, 512, 2048), BF16), pltpu.VMEM((2048, N), BF16), pltpu.VMEM((4, 512, N), BF16),
            pltpu.VMEM((2, 256, N), BF16), pltpu.VMEM((2, 512, N), BF16),
            pltpu.VMEM((4, 4, 2, 4, 8, N), BF16), pltpu.VMEM((N, N), BF16), pltpu.VMEM((N, N), F32),
            pltpu.VMEM((N, terms), BF16), pltpu.VMEM((terms, N), BF16), pltpu.VMEM((128, 128), F32),
            pltpu.VMEM((512, N), BF16), pltpu.VMEM((512, N), BF16), pltpu.VMEM((N, N), F32),
            pltpu.VMEM((16, 4, 8, N), BF16), pltpu.VMEM((16, 4, 8, N), BF16), pltpu.VMEM((4, 4, 4, 8, N), BF16),
            pltpu.VMEM((3, 4, 4, 8, N), BF16), pltpu.VMEM((4, 4, 8, N), BF16), pltpu.VMEM((3, 4, 8, N), BF16),
            pltpu.VMEM((4, 8, N), BF16), pltpu.VMEM((3, 8, N), BF16), pltpu.VMEM((8, N), F32),
            pltpu.VMEM((2, 8, 128), F32), pltpu.VMEM((22, 8, 128), F32),
            dma((4,)), dma, dma((3,)), dma((3,)), dma((2, 3)), dma((2, 3)), dma((3, 3)), dma((3, 3)), dma((2,)), dma((2,)),
            dma((2,)), dma((2,)), dma((2,)), dma((2,)), dma((2, 2)), dma((2, 2))],
        compiler_params=pltpu.CompilerParams(
            collective_id=0, has_side_effects=True, vmem_limit_bytes=56 * 2**20),
    )(activations, whitening, factor)


def solution(mesh):
    placed = (P("dp", "tensor"), P("tensor", None), P(("dp", "tensor"), None))
    return jax.shard_map(
        shards, mesh=mesh, in_specs=placed, out_specs=P(("dp", "tensor"), None), check_vma=False
    )
```

```python
import jax, jax.numpy as jnp
from jax import lax
from jax.sharding import PartitionSpec as P
from jax.experimental import pallas as pl
from jax.experimental.pallas import tpu as pltpu

F32, BF16 = jnp.float32, jnp.bfloat16
HI = lax.Precision.HIGHEST

def over_lanes(x, j):
    return jnp.broadcast_to(x[:, j:j + 1], (8, 128))

def over_sublanes(x, j):
    return jnp.broadcast_to(x[j:j + 1, :], (8, 128))

def tree(p):
    while len(p) > 1:
        p = [p[i] + p[i + 1] for i in range(0, len(p), 2)]
    return p[0]

def eliminate(rows, cols, first, s, lane, sub):
    base = first + 8 * s
    more = s + 1 < len(rows)
    inside = (lane >= base) & (lane < base + 8)
    panel = rows[s]
    if cols is None:
        cols = [over_lanes(panel, base + j) for j in range(8)]
    cols = list(cols)
    z = jnp.where(inside, jnp.where(lane - base == sub, 1.0, 0.0), panel)
    ahead = [over_lanes(panel, base + 8 + j) for j in range(8)] if more else []
    for m in range(4):
        a, b = 2 * m, 2 * m + 1
        ea, eb = cols[a], cols[b]
        g00, g10 = over_sublanes(ea, a), over_sublanes(ea, b)
        g01, g11 = over_sublanes(eb, a), over_sublanes(eb, b)
        r = 1.0 / (g00 * g11 - g01 * g10)
        q00, q01, q10, q11 = g11 * r, -(g01 * r), -(g10 * r), g00 * r
        fa = -(ea * q00 + eb * q10)
        fb = -(ea * q01 + eb * q11)
        fa = jnp.where(sub == a, q00, jnp.where(sub == b, q10, fa))
        fb = jnp.where(sub == a, q01, jnp.where(sub == b, q11, fb))
        pair = (sub == a) | (sub == b)

        def step(v):
            return (jnp.where(pair, 0.0, v) + fa * over_sublanes(v, a)) + fb * over_sublanes(v, b)

        for c in range(b + 1, 8):
            cols[c] = step(cols[c])
        z = step(z)
        ahead = [step(v) for v in ahead]
    following = None
    trow = [over_sublanes(z, j) for j in range(8)]
    for i in list(range(s + 1, len(rows))) + list(range(s)):
        v = rows[i]
        spread = [over_lanes(v, base + j) for j in range(8)]
        if i == s + 1:
            following = [
                over_lanes(v, base + 8 + j) - tree([spread[m] * over_sublanes(ahead[j], m) for m in range(8)])
                for j in range(8)]
        rows[i] = jnp.where(inside, 0.0, v) - tree([spread[j] * trow[j] for j in range(8)])
    rows[s] = z
    return following

def product(a, b):
    a1 = a.astype(BF16)
    a2 = (a - a1.astype(F32)).astype(BF16)
    b1 = b.astype(BF16)
    b2 = (b - b1.astype(F32)).astype(BF16)
    left = jnp.concatenate([a1, a1, a2, a2], axis=1)
    right = jnp.concatenate([b1, b2, b1, b2], axis=0)
    return jnp.dot(left, right, preferred_element_type=F32)

def invert_block(rows, size, fill):
    lane = lax.broadcasted_iota(jnp.int32, (8, 128), 1)
    sub = lax.broadcasted_iota(jnp.int32, (8, 128), 0)
    each = size // 8
    groups = 128 // size
    zero = [jnp.zeros((8, 128), F32)]
    for g in range(groups):
        own = rows[each * g:each * g + each]
        cols = None
        for s in range(each):
            cols = eliminate(own, cols, size * g, s, lane, sub)
            fill()
        rows[each * g:each * g + each] = own
        inside = (lane >= size * g) & (lane < size * g + size)
        t = jnp.concatenate(zero * (each * g) + own + zero * (16 - each * g - each), axis=0)
        for o in [(g + e) % groups for e in range(1, groups)]:
            c = jnp.concatenate([jnp.where(inside, rows[i], 0.0) for i in range(each * o, each * o + each)], axis=0)
            u = product(c, t)
            for n in range(each):
                i = each * o + n
                rows[i] = jnp.where(inside, 0.0, rows[i]) - u[8 * n:8 * n + 8]
    return rows

TERMS = ((0, 0), (0, 1), (1, 0), (1, 1))
SIZE = 64
N = 1024
LAST = N - 128

def split(x):
    one = x.astype(BF16)
    rest = x - one.astype(F32)
    two = rest.astype(BF16)
    three = (rest - two.astype(F32)).astype(BF16)
    return one, two, three

def hadamard_block(f_ref, i, rows, j, cols):
    g = lax.dot_general(f_ref[:, i:i + rows], f_ref[:, j:j + cols], (((0,), (0,)), ((), ())), preferred_element_type=F32)
    row = lax.broadcasted_iota(jnp.int32, (rows, cols), 0) + i
    col = lax.broadcasted_iota(jnp.int32, (rows, cols), 1) + j
    return g * g + jnp.where(row == col, 0.1, 0.0)

def invert(f_ref, inv_ref, left, right, pivot, between):
    def run(todo, rate):
        def fill():
            for _ in range(rate):
                if todo:
                    todo.pop(0)()
        return fill

    def fill_rows(j):
        def go():
            inv_ref[128 * j:128 * j + 128, :] = hadamard_block(f_ref, 128 * j, 128, 0, N)
        return go

    d = hadamard_block(f_ref, 0, 128, 0, 128)
    todo = [fill_rows(j) for j in range(8)]
    first = invert_block([d[8 * i:8 * i + 8] for i in range(16)], SIZE, run(todo, 1))
    pivot[...] = jnp.concatenate(first, axis=0)

    def work(k0):
        p = pivot[...]
        row = lax.broadcasted_iota(jnp.int32, (N, 128), 0)
        col = lax.broadcasted_iota(jnp.int32, (128, 256), 1)
        own = (row >= k0) & (row < k0 + 128)
        pp = jnp.concatenate([p, p], axis=1)

        def panel(j):
            def go():
                cols = slice(256 * j, 256 * j + 256)
                t = product(p, inv_ref[pl.ds(k0, 128), cols])
                at = col + 256 * j
                t = jnp.where((at >= k0) & (at < k0 + 128), pp, t)
                inv_ref[pl.ds(k0, 128), cols] = t
                tt = split(t)
                for i, (a, b) in enumerate(TERMS):
                    right[128 * i:128 * i + 128, cols] = tt[b]
            return go

        def column():
            old = inv_ref[:, pl.ds(k0, 128)]
            cc = split(jnp.where(own, 0.0, old))
            for i, (a, b) in enumerate(TERMS):
                left[:, 128 * i:128 * i + 128] = cc[a]
            inv_ref[:, pl.ds(k0, 128)] = jnp.where(own, old, 0.0)

        def update(r, c):
            def go():
                rows, cols = slice(128 * r, 128 * r + 128), slice(512 * c, 512 * c + 512)
                inv_ref[rows, cols] -= jnp.dot(left[rows, :], right[:, cols], preferred_element_type=F32)
            return go

        return [column] + [panel(j) for j in range(4)] + [update(r, c) for r in range(8) for c in range(2)]

    def step(k, carry):
        between(k)
        k0 = pl.multiple_of(k * 128, 128)
        n0 = pl.multiple_of(k * 128 + 128, 128)
        p = pivot[...]
        tn = product(p, inv_ref[pl.ds(k0, 128), pl.ds(n0, 128)])
        d = inv_ref[pl.ds(n0, 128), pl.ds(n0, 128)] - product(
            inv_ref[pl.ds(n0, 128), pl.ds(k0, 128)], tn)
        todo = work(k0)
        nxt = invert_block([d[8 * i:8 * i + 8] for i in range(16)], SIZE, run(todo, 2))
        while todo:
            todo.pop(0)()
        pivot[...] = jnp.concatenate(nxt, axis=0)
        return carry

    lax.fori_loop(0, N // 128 - 1, step, 0)


MESH = pl.DeviceIdType.MESH
PARTS = ((0, 384, (0, 1, 2)), (384, 384, (1, 2, 0)), (768, 256, (2, 0, 1)))
STAGES = (3, 4, 5, 6, None)


def ring(i):
    return [i] + [jnp.where(i + s >= 4, i + s - 4, i + s) for s in (1, 2, 3)]


class Map:
    def __init__(self):
        dp, z = lax.axis_index("dp"), lax.axis_index("tensor")
        self.c = dp % 2
        self.at = (dp // 8, (dp // 2) % 4, z)
        self.rings = [ring(i) for i in self.at]
        self.partner = self.name(self.at, 1 - self.c)

    def name(self, at, core):
        return ((at[0] * 4 + at[1]) * 2 + core, at[2])

    def peer(self, axis, s):
        at = list(self.at)
        at[axis] = self.rings[axis][s]
        return self.name(at, self.c)

    def close(self):
        x, y, _ = self.at
        zs = self.rings[2]
        return [self.name((x, y, zs[s]), core) for core in (self.c, 1 - self.c) for s in range(4) if core is not self.c or s]

    def plane(self):
        xs, ys, _ = self.rings
        return [self.name((xs[a], ys[b], self.at[2]), self.c) for a in range(4) for b in range(4) if a + b]


def greet(m):
    barrier = pltpu.get_barrier_semaphore()
    for device in m.close() + m.plane():
        pl.semaphore_signal(barrier, inc=1, device_id=device, device_id_type=MESH)
    return barrier


def remote(src, dst, send, recv, device):
    return pltpu.make_async_remote_copy(
        src_ref=src, dst_ref=dst, send_sem=send, recv_sem=recv, device_id=device, device_id_type=MESH)


def all_of(ref, sem):
    return pltpu.make_async_copy(ref, ref, sem)


def whole_kernel(act_ref, wh_ref, f_ref, out_ref,
                 act, wh, part, far, near, f5, factor, inv, left, right, pivot, summed, squared, moment,
                 core_out, core_in, mine, in1, out2, in2, out3, in3, total, norm_out, norm_in,
                 act_sem, wh_sem, f_send, f_recv, l_send, l_recv, s_send, s_recv, n_send, n_recv,
                 pair_send, pair_recv, far_send, far_recv, near_send, near_recv):
    m = Map()
    c = m.c
    x, y, z = m.at
    barrier = greet(m)
    zs = m.rings[2]
    order = (zs[2], zs[1], zs[3], z)

    def load(r):
        rows = pl.ds(pl.multiple_of(order[r] * 512, 512), 512)
        return pltpu.make_async_copy(act_ref.at[rows, :], act.at[r], act_sem.at[r])

    load_wh = pltpu.make_async_copy(wh_ref, wh, wh_sem)
    load_wh.start()
    for r in range(4):
        load(r).start()
    f5[x, y, c, z] = f_ref[...]
    pl.semaphore_wait(barrier, 22)

    first, second = pl.ds(0, 512), pl.ds(512, 512)
    hops = [
        (f_ref, f5.at[x, y, c, z], 2, f5.at[0, 0, 0, pl.ds(0, 3)]),
        (f5.at[x, y, c, :, :, first], f5.at[x, y, c, :, :, first], 0, f5.at[pl.ds(0, 3), 0, 0, :, :, first]),
        (f5.at[x, y, c, :, :, second], f5.at[x, y, c, :, :, second], 1, f5.at[pl.ds(0, 3), 0, 0, :, :, first]),
    ]

    def hop_start(i):
        src, dst, axis, _ = hops[i]
        for s in (2, 1, 3):
            remote(src, dst, f_send.at[i], f_recv.at[i], m.peer(axis, s)).start()

    def hop_end(i, sems):
        all_of(hops[i][3], sems.at[i]).wait()

    def strip(half, s):
        if half == 0:
            return f5.at[:, m.rings[1][s], c, :, :, first]
        return f5.at[x, :, c, :, :, second] if s == 0 else f5.at[m.rings[0][s], :, c, :, :, second]

    def last_hop(half, s):
        return remote(strip(half, 0), strip(half, 0), l_send.at[half, s - 1], l_recv.at[half, s - 1], m.peer(1 - half, s))

    def pair(half, s):
        return remote(strip(half, s), strip(half, s), pair_send.at[0], pair_recv.at[0], m.partner)

    hop_start(0)

    up, down = m.peer(2, 1), m.peer(2, 3)
    far_up = remote(part.at[0, pl.ds(0, 256)], far.at[0], far_send.at[0], far_recv.at[0], up)
    far_down = remote(part.at[0, pl.ds(256, 256)], far.at[1], far_send.at[1], far_recv.at[1], down)

    def near_copy(slot, half):
        rows = pl.ds(256 * half, 256)
        return remote(part.at[1 + slot, rows], near.at[slot, rows], near_send.at[slot, half], near_recv.at[slot, half],
                      down if slot else up)

    load_wh.wait()
    for r in range(4):
        load(r).wait()

        def tile(i, carry, r=r):
            cols = pl.ds(pl.multiple_of(i * 256, 256), 256)
            part[r, :, cols] = jnp.dot(act[r], wh[:, cols], preferred_element_type=F32).astype(BF16)
            return carry

        def half_tile(i, carry, r=r):
            rows = pl.ds(pl.multiple_of((i // 4) * 256, 256), 256)
            cols = pl.ds(pl.multiple_of((i % 4) * 256, 256), 256)
            part[r, rows, cols] = jnp.dot(act[r, rows, :], wh[:, cols], preferred_element_type=F32).astype(BF16)
            return carry

        if r == 0:
            lax.fori_loop(0, 4, half_tile, 0)
            far_up.start()
            lax.fori_loop(4, 8, half_tile, 0)
            far_down.start()
        else:
            lax.fori_loop(0, 4, tile, 0)
        if r == 0:
            hop_end(0, f_recv)
            hop_start(1)
            hop_start(2)
        if r == 1:
            hop_end(1, f_recv)
            hop_end(2, f_recv)
            for s in (2, 1, 3):
                for half in (0, 1):
                    last_hop(half, s).start()
            for half in (0, 1):
                pair(half, 0).start()
            near_copy(0, 1).start()
        if r == 2:
            near_copy(1, 0).start()
        if r == 3:
            for s in (1, 3, 2):
                for half in (0, 1):
                    last_hop(half, s).wait_recv()
                    pair(half, 4 - s).start()

    def forward(copy_in, slot):
        begin = 256 * slot
        copy_in.wait_recv()

        def add(i, carry):
            here = pl.ds(pl.multiple_of(i * 32, 32), 32)
            rows = pl.ds(pl.multiple_of(begin + i * 32, 32), 32)
            part[1 + slot, rows, :] = (part[1 + slot, rows, :].astype(F32) + far[slot, here, :].astype(F32)).astype(BF16)
            return carry

        lax.fori_loop(0, 8, add, 0)
        near_copy(slot, slot).start()

    forward(far_up, 0)
    forward(far_down, 1)
    all_of(f5.at[:, :, 0], pair_recv.at[0]).wait()

    def flatten(i, carry):
        for e in range(2):
            for h in range(2):
                block = jnp.concatenate(
                    [f5[i // 4, i % 4, e, 2 * h].astype(F32), f5[i // 4, i % 4, e, 2 * h + 1].astype(F32)], axis=0)
                factor[pl.ds(pl.multiple_of(i * 64 + 32 * e + 16 * h, 16), 16), :] = block.astype(BF16)
        return carry

    lax.fori_loop(0, 16, flatten, 0)

    across = remote(core_out, core_in, pair_send.at[1], pair_recv.at[1], m.partner)

    def rows_of(i, core):
        return pl.ds(pl.multiple_of((i * 2 + core) * 32, 32), 32)

    def stage_moment():
        for slot in (0, 1):
            for half in (0, 1):
                near_copy(slot, half).wait_recv()

        def add(i, carry):
            rows = pl.ds(pl.multiple_of(i * 32, 32), 32)
            summed[rows, :] = (part[3, rows, :].astype(F32) + near[0, rows, :].astype(F32)
                               + near[1, rows, :].astype(F32)).astype(BF16)
            return carry

        lax.fori_loop(0, 16, add, 0)

        def project(i, carry):
            cols = pl.ds(pl.multiple_of(i * 512, 512), 512)
            p = jnp.dot(summed[...], factor[:, cols], preferred_element_type=F32)
            squared[:, cols] = (p * p).astype(BF16)
            return carry

        lax.fori_loop(0, 2, project, 0)

        def moments(i, carry):
            rows = pl.ds(pl.multiple_of(i * 256, 256), 256)
            moment[rows, :] = lax.dot_general(
                summed[:, rows], squared[...], (((0,), (0,)), ((), ())), preferred_element_type=F32)
            return carry

        lax.fori_loop(0, 4, moments, 0)

        def cast(i, carry):
            core_out[i] = moment[rows_of(i, 1 - c), :].reshape(4, 8, N).astype(BF16)
            return carry

        lax.fori_loop(0, 16, cast, 0)
        across.start()

    def pick(ref, fixed, cols):
        index = [fixed.get(axis, slice(None)) for axis in range(3)]
        return ref.at[(*index, slice(None), pl.ds(cols[0], cols[1]))]

    def send1(p, s):
        lo, width, (a, b, e) = PARTS[p]
        src = pick(mine, {a: m.rings[a][s]}, (lo, width))
        return remote(src, in1.at[s - 1, :, :, :, pl.ds(lo, width)], s_send.at[0, p], s_recv.at[0, p], m.peer(a, s))

    def send2(p, s):
        lo, width, (a, b, e) = PARTS[p]
        src = out2.at[m.rings[b][s], :, :, pl.ds(lo, width)]
        return remote(src, in2.at[s - 1, :, :, pl.ds(lo, width)], s_send.at[1, p], s_recv.at[1, p], m.peer(b, s))

    def send3(p, s):
        lo, width, (a, b, e) = PARTS[p]
        src = out3.at[m.rings[e][s], :, pl.ds(lo, width)]
        return remote(src, in3.at[s - 1, :, pl.ds(lo, width)], s_send.at[2, p], s_recv.at[2, p], m.peer(e, s))

    def landed(level, p, sems):
        lo, width, _ = PARTS[p]
        ref = (in1.at[:, :, :, :, pl.ds(lo, width)], in2.at[:, :, :, pl.ds(lo, width)], in3.at[:, :, pl.ds(lo, width)])[level]
        all_of(ref, sems.at[level, p]).wait()

    def stage_cores():
        across.wait_recv()

        def add(i, carry):
            block = moment[rows_of(i, c), :].reshape(4, 8, N) + core_in[i].astype(F32)
            moment[rows_of(i, c), :] = block.reshape(32, N)
            mine[i // 4, i % 4] = block.astype(BF16)
            return carry

        lax.fori_loop(0, 16, add, 0)
        for s in (2, 1, 3):
            for p in range(3):
                send1(p, s).start()

    def gather_sum(row, many, cols, blocks):
        rows = pl.ds(pl.multiple_of(row, 8), 8 * many)
        t = moment[rows, cols]
        for block in blocks:
            t = t + block.astype(F32).reshape(8 * many, cols.size)
        moment[rows, cols] = t
        return t.astype(BF16).reshape(many, 8, cols.size)

    def row_at(ix, iy, iz):
        return (((ix * 4 + iy) * 2 + c) * 4 + iz) * 8

    def stage_one():
        spans = [pl.ds(lo, width) for lo, width, _ in PARTS]
        landed(0, 0, s_recv)

        def add_x(i, carry):
            out2[i, :, :, spans[0]] = gather_sum(
                row_at(x, i, 0), 4, spans[0], [in1[s, i, :, :, spans[0]] for s in range(3)])
            return carry

        lax.fori_loop(0, 4, add_x, 0)
        for s in (2, 1, 3):
            send2(0, s).start()
        landed(0, 1, s_recv)

        def add_y(i, carry):
            out2[:, i, :, spans[1]] = gather_sum(
                row_at(i, y, 0), 4, spans[1], [in1[s, i, :, :, spans[1]] for s in range(3)])
            return carry

        lax.fori_loop(0, 4, add_y, 0)
        for s in (2, 1, 3):
            send2(1, s).start()
        landed(0, 2, s_recv)

        def add_z(i, carry):
            for j in range(4):
                out2[i, pl.ds(j, 1), :, spans[2]] = gather_sum(
                    row_at(i, j, z), 1, spans[2], [in1[s, i, j, :, spans[2]] for s in range(3)])
            return carry

        lax.fori_loop(0, 4, add_z, 0)
        for s in (2, 1, 3):
            send2(2, s).start()

    def stage_two():
        spans = [pl.ds(lo, width) for lo, width, _ in PARTS]
        landed(1, 0, s_recv)
        out3[:, :, spans[0]] = gather_sum(row_at(x, y, 0), 4, spans[0], [in2[s, :, :, spans[0]] for s in range(3)])
        for s in (2, 1, 3):
            send3(0, s).start()
        for p in (1, 2):
            landed(1, p, s_recv)
            for i in range(4):
                row = row_at(i, y, z) if p == 1 else row_at(x, i, z)
                out3[pl.ds(i, 1), :, spans[p]] = gather_sum(row, 1, spans[p], [in2[s, i, :, spans[p]] for s in range(3)])
            for s in (2, 1, 3):
                send3(p, s).start()

    def stage_three():
        own = pl.multiple_of((((x * 4 + y) * 2 + c) * 4 + z) * 8, 8)
        for p in range(3):
            lo, width, _ = PARTS[p]
            cols = pl.ds(lo, width)
            landed(2, p, s_recv)
            t = moment[pl.ds(own, 8), cols]
            for s in range(3):
                t = t + in3[s, :, cols].astype(F32)
            total[:, cols] = t

    stages = (stage_moment, stage_cores, stage_one, stage_two, stage_three)

    def between(k):
        for stage, when in zip(stages, STAGES):
            if when is not None:
                pl.when(k == when)(stage)

    invert(factor, inv, left, right, pivot, between)
    for stage, when in zip(stages, STAGES):
        if when is None:
            stage()
    moved = jnp.where(lax.broadcasted_iota(jnp.int32, (8, N), 1) < LAST, total[...], 0.0)
    stacked = jnp.concatenate([piece.astype(F32) for piece in split(moved)], axis=0).astype(BF16)
    partly = jnp.zeros((8, N), F32)
    for piece in split(inv[...])[:2]:
        products = jnp.dot(stacked, piece, preferred_element_type=F32)
        partly = partly + ((products[16:24] + products[8:16]) + products[0:8])
    corner = jnp.dot(total[:, LAST:] - partly[:, LAST:], pivot[...], precision=HI, preferred_element_type=F32)
    others = partly[:, :LAST] + jnp.dot(corner, inv[LAST:, :LAST], precision=HI, preferred_element_type=F32)
    updated = jnp.concatenate([others, corner], axis=1)

    squares = jnp.sum(updated * updated, axis=0, keepdims=True)
    for j in range(8):
        norm_out[0, j:j + 1, :] = squares[:, 128 * j:128 * j + 128]
    close, plane = m.close(), m.plane()
    for i, device in enumerate(close):
        remote(norm_out.at[0], norm_in.at[i], n_send.at[0], n_recv.at[0], device).start()
    all_of(norm_in.at[pl.ds(0, 7)], n_recv.at[0]).wait()
    norm = tree([norm_out[0]] + [norm_in[i] for i in range(7)])
    norm_out[1] = norm
    for i, device in enumerate(plane):
        remote(norm_out.at[1], norm_in.at[7 + i], n_send.at[1], n_recv.at[1], device).start()
    all_of(norm_in.at[pl.ds(7, 15)], n_recv.at[1]).wait()
    norm = tree([norm] + [norm_in[7 + i] for i in range(15)])
    scale = jnp.sqrt(norm * (1.0 / N) + 1e-6)
    for j in range(8):
        cols = slice(128 * j, 128 * j + 128)
        out_ref[:, cols] = updated[:, cols] / scale[j:j + 1, :]

    for i in range(3):
        hop_end(i, f_send)
    for s in (2, 1, 3):
        for half in (0, 1):
            last_hop(half, s).wait_send()
    for level in range(3):
        for p in range(3):
            landed(level, p, s_send)
    all_of(norm_in.at[pl.ds(0, 7)], n_send.at[0]).wait()
    all_of(norm_in.at[pl.ds(7, 15)], n_send.at[1]).wait()
    all_of(f5.at[:, :, 0], pair_send.at[0]).wait()
    for slot in (0, 1):
        for half in (0, 1):
            near_copy(slot, half).wait_send()
    for copy in (across, far_up, far_down):
        copy.wait_send()


def shards(activations, whitening, factor):
    terms = 128 * len(TERMS)
    dma = pltpu.SemaphoreType.DMA
    return pl.pallas_call(
        whole_kernel,
        out_shape=jax.ShapeDtypeStruct((8, N), F32),
        in_specs=[pl.BlockSpec(memory_space=pl.ANY)] * 2 + [pl.BlockSpec(memory_space=pltpu.VMEM)],
        out_specs=pl.BlockSpec(memory_space=pltpu.VMEM),
        scratch_shapes=[
            pltpu.VMEM((4, 512, 2048), BF16), pltpu.VMEM((2048, N), BF16), pltpu.VMEM((4, 512, N), BF16),
            pltpu.VMEM((2, 256, N), BF16), pltpu.VMEM((2, 512, N), BF16),
            pltpu.VMEM((4, 4, 2, 4, 8, N), BF16), pltpu.VMEM((N, N), BF16), pltpu.VMEM((N, N), F32),
            pltpu.VMEM((N, terms), BF16), pltpu.VMEM((terms, N), BF16), pltpu.VMEM((128, 128), F32),
            pltpu.VMEM((512, N), BF16), pltpu.VMEM((512, N), BF16), pltpu.VMEM((N, N), F32),
            pltpu.VMEM((16, 4, 8, N), BF16), pltpu.VMEM((16, 4, 8, N), BF16), pltpu.VMEM((4, 4, 4, 8, N), BF16),
            pltpu.VMEM((3, 4, 4, 8, N), BF16), pltpu.VMEM((4, 4, 8, N), BF16), pltpu.VMEM((3, 4, 8, N), BF16),
            pltpu.VMEM((4, 8, N), BF16), pltpu.VMEM((3, 8, N), BF16), pltpu.VMEM((8, N), F32),
            pltpu.VMEM((2, 8, 128), F32), pltpu.VMEM((22, 8, 128), F32),
            dma((4,)), dma, dma((3,)), dma((3,)), dma((2, 3)), dma((2, 3)), dma((3, 3)), dma((3, 3)), dma((2,)), dma((2,)),
            dma((2,)), dma((2,)), dma((2,)), dma((2,)), dma((2, 2)), dma((2, 2))],
        compiler_params=pltpu.CompilerParams(
            collective_id=0, has_side_effects=True, vmem_limit_bytes=56 * 2**20),
    )(activations, whitening, factor)


def solution(mesh):
    placed = (P("dp", "tensor"), P("tensor", None), P(("dp", "tensor"), None))
    return jax.shard_map(
        shards, mesh=mesh, in_specs=placed, out_specs=P(("dp", "tensor"), None), check_vma=False
    )
```
